32 devices in a mesh: ctx: 8 (over z, y), fsdp: 4 (over x, core).
Axes of the slice: x: 2, y: 2, z: 4, core: 2. Of those that a mesh axis runs over, the one named last changes fastest.
Arguments:
- block_input: float32 [4, 1024, 960], P('fsdp', 'ctx'), may hold values from -20 to 20
- pair_of_device: int32 [8], replicated, may hold values from 0 to 7, each once
- query_weight: bfloat16 [1, 960, 960], P(None, 'fsdp'), may hold values from -0.1875 to 0.1875
- key_weight: bfloat16 [1, 960, 320], P(None, 'fsdp'), may hold values from -0.1875 to 0.1875
- value_matrix: bfloat16 [1, 960, 320], P(None, 'fsdp'), may hold values from -0.1875 to 0.1875
- output_weight: bfloat16 [1, 960, 960], P(None, None, 'fsdp'), may hold values from -0.75 to 0.75
- gate_weight: bfloat16 [1, 960, 2560], P(None, 'fsdp'), may hold values from -0.1875 to 0.1875
- up_weight: bfloat16 [1, 960, 2560], P(None, 'fsdp'), may hold values from -0.1875 to 0.1875
- down_weight: bfloat16 [1, 2560, 960], P(None, None, 'fsdp'), may hold values from -0.125 to 0.125
- attention_gain: float32 [1, 960], replicated, may hold values from 0.5 to 1.5
- feedforward_gain: float32 [1, 960], replicated, may hold values from 0.5 to 1.5
- output_cotangent: float32 [4, 1024, 960], P('fsdp', 'ctx'), may hold values from -6 to 6
Outputs:
- block_output: float32 [4, 1024, 960], P('fsdp', 'ctx')
- input_grad: float32 [4, 1024, 960], P('fsdp', 'ctx')
- query_weight_grad: float32 [1, 960, 960], P(None, 'fsdp', 'ctx')
- key_weight_grad: float32 [1, 960, 320], P(None, 'fsdp', 'ctx')
- value_weight_grad: float32 [1, 960, 320], P(None, 'fsdp', 'ctx')
- output_weight_grad: float32 [1, 960, 960], P(None, 'ctx', 'fsdp')
- gate_weight_grad: float32 [1, 960, 2560], P(None, 'fsdp', 'ctx')
- up_weight_grad: float32 [1, 960, 2560], P(None, 'fsdp', 'ctx')
- down_weight_grad: float32 [1, 2560, 960], P(None, 'ctx', 'fsdp')
- attention_gain_grad: float32 [1, 960], replicated
- feedforward_gain_grad: float32 [1, 960], replicated
The draws below stay inside these ranges and needn't reach their ends.
All inputs are finite; a program needn't handle non-finite values.
Results may differ from the reference program's by a relative error of at most 0.024.
Values may be sent and summed in bfloat16 or wider, within the bound.
No kernel may reach another device: no remote copies, remote signals or barrier semaphores. Data moves between devices by JAX's collectives and lax.ppermute only.
A program may use at most 192 MiB of HBM per device.

```python
import math
import jax
import jax.numpy as jnp
from jax import lax

MODEL_WIDTH = 960
QUERY_HEADS = 15
KEY_HEADS = 5
HEAD_SIZE = 64
FF = 2560
DECODER_LAYERS = 1
BLK = 64
SEQ = 1024
SEQS = 4
N_CTX = 8


def draw_block_input(key, part):
    base_key = jax.random.fold_in(key, 1)
    scale_key = jax.random.fold_in(key, 2)
    unscaled = jnp.clip(jax.random.normal(base_key, (SEQS, SEQ, MODEL_WIDTH), jnp.float32), -5.0, 5.0)
    factors = jnp.exp(jax.random.uniform(scale_key, (SEQS, SEQ, 1), jnp.float32, math.log(0.4), math.log(4.0)))
    return unscaled * factors


def block_levels(rng, dims, shards, smallest, largest):
    level = 1.0
    for dim, shards_of in shards:
        draws = jax.random.uniform(jax.random.fold_in(jax.random.fold_in(rng, 6), dim), (shards_of,), jnp.float32, smallest / len(shards), largest / len(shards))
        level = level * jnp.repeat(jnp.exp(draws), dims[dim] // shards_of).reshape((-1,) + (1,) * (len(dims) - 1 - dim))
    return level


def noise(stream_key, shape, scale, most, pieces=(), held_as=jnp.bfloat16):
    loudness = block_levels(stream_key, shape, pieces, -0.22, 0.18) if pieces else 1.0
    values = jax.random.normal(stream_key, shape, jnp.float32) * scale * loudness
    return jnp.minimum(jnp.maximum(values, -most), most).astype(held_as)


def setup_inputs(seed: int = 0) -> dict:
    keys = jax.random.split(jax.random.key(seed), 13)
    block_input = draw_block_input(jax.random.fold_in(keys[12], 71), 0)
    pair_of_device = jax.random.permutation(keys[1], N_CTX).astype(jnp.int32)
    query_weight = noise(keys[2], (DECODER_LAYERS, MODEL_WIDTH, QUERY_HEADS * HEAD_SIZE), MODEL_WIDTH ** -0.5, 0.1875, ((1, 4),))
    key_weight = noise(keys[3], (DECODER_LAYERS, MODEL_WIDTH, KEY_HEADS * HEAD_SIZE), MODEL_WIDTH ** -0.5, 0.1875, ((1, 4),))
    value_matrix = noise(keys[4], (DECODER_LAYERS, MODEL_WIDTH, KEY_HEADS * HEAD_SIZE), MODEL_WIDTH ** -0.5, 0.1875, ((1, 4),))
    output_weight = noise(keys[5], (DECODER_LAYERS, QUERY_HEADS * HEAD_SIZE, MODEL_WIDTH), HEAD_SIZE ** -0.5, 0.75, ((2, 4),))
    gate_weight = noise(keys[6], (DECODER_LAYERS, MODEL_WIDTH, FF), MODEL_WIDTH ** -0.5, 0.1875, ((1, 4),))
    up_weight = noise(keys[7], (DECODER_LAYERS, MODEL_WIDTH, FF), MODEL_WIDTH ** -0.5, 0.1875, ((1, 4),))
    down_weight = noise(keys[8], (DECODER_LAYERS, FF, MODEL_WIDTH), FF ** -0.5, 0.125, ((2, 4),))
    attention_gain = jnp.clip(1.0 + 0.1 * jax.random.normal(keys[9], (DECODER_LAYERS, MODEL_WIDTH), jnp.float32), 0.5, 1.5)
    feedforward_gain = jnp.clip(1.0 + 0.1 * jax.random.normal(keys[10], (DECODER_LAYERS, MODEL_WIDTH), jnp.float32), 0.5, 1.5)
    output_cotangent = noise(keys[11], (SEQS, SEQ, MODEL_WIDTH), 1.0, 6.0, ((0, 4), (1, 8)), jnp.float32)
    return {"block_input": block_input, "pair_of_device": pair_of_device, "query_weight": query_weight, "key_weight": key_weight, "value_matrix": value_matrix, "output_weight": output_weight, "gate_weight": gate_weight, "up_weight": up_weight, "down_weight": down_weight, "attention_gain": attention_gain, "feedforward_gain": feedforward_gain, "output_cotangent": output_cotangent}


EPSILON = 1e-05
THETA = 100000.0
QUERY_BLOCK = 512

def convert_to_half(values):
    return lax.optimization_barrier(values.astype(jnp.bfloat16))

def matrix_product(left, right):
    return jnp.dot(left, right, preferred_element_type=jnp.float32)

def key_positions(pair_of_device):
    within = jnp.arange(BLK, dtype=jnp.int32)
    early_blocks = pair_of_device[:, None] * BLK + within[None, :]
    late_blocks = (2 * N_CTX - 1 - pair_of_device)[:, None] * BLK + within[None, :]
    return jnp.concatenate([early_blocks, late_blocks], axis=1).reshape(-1).astype(jnp.int32)

def rope_tables(positions):
    half_size = HEAD_SIZE // 2
    frequency = jnp.exp(jnp.arange(half_size, dtype=jnp.float32) * (-2.0 * math.log(THETA) / HEAD_SIZE))
    angles = positions.astype(jnp.float32)[:, None] * frequency[None, :]
    return (jnp.cos(angles), jnp.sin(angles))

def apply_rotation(values, cosine_values, sine_values):
    half_size = values.shape[-1] // 2
    former = values[..., :half_size]
    latter = values[..., half_size:]
    cosine = cosine_values[:, None, :]
    sine_part = sine_values[:, None, :]
    return jnp.concatenate([former * cosine - latter * sine_part, latter * cosine + former * sine_part], axis=-1)

def inverse_rotation(values, cosine_values, sine_values):
    half_size = values.shape[-1] // 2
    former = values[..., :half_size]
    latter = values[..., half_size:]
    cosine = cosine_values[:, None, :]
    sine_part = sine_values[:, None, :]
    return jnp.concatenate([former * cosine + latter * sine_part, latter * cosine - former * sine_part], axis=-1)

def norm_forward(hidden, gain):
    factor = lax.rsqrt(lax.optimization_barrier(jnp.mean(hidden * hidden, axis=-1, keepdims=True)) + EPSILON)
    normed = hidden * factor
    return (normed, factor, convert_to_half(normed * gain))

def norm_backward(grad_out, normed, factor, gain):
    grad_gain = lax.optimization_barrier(jnp.sum(grad_out * normed, axis=0))
    scaled = grad_out * gain
    return (factor * (scaled - normed * lax.optimization_barrier(jnp.mean(scaled * normed, axis=-1, keepdims=True))), grad_gain)

def attend(query_rows, heads_of_keys, heads_of_values, positions):
    count_of_rows = query_rows.shape[0]
    rows_per_block = min(QUERY_BLOCK, count_of_rows)
    query_groups = QUERY_HEADS // KEY_HEADS
    key_float = heads_of_keys.astype(jnp.float32)
    value_float = heads_of_values.astype(jnp.float32)
    scale = 1.0 / math.sqrt(HEAD_SIZE)

    def one_block(block_index):
        start_offset = block_index * rows_per_block
        block_of_queries = lax.dynamic_slice_in_dim(query_rows, start_offset, rows_per_block, 0).astype(jnp.float32).reshape(rows_per_block, KEY_HEADS, query_groups, HEAD_SIZE)
        current = lax.dynamic_slice_in_dim(positions, start_offset, rows_per_block, 0)
        visible = positions[None, :] <= current[:, None]
        scores = jnp.einsum('qhgd,khd->hgqk', block_of_queries, key_float) * scale
        scores = jnp.where(visible[None, None], scores, -1e+30)
        highest = lax.optimization_barrier(jnp.max(scores, axis=-1, keepdims=True))
        raised = jnp.exp(scores - highest)
        total = lax.optimization_barrier(jnp.sum(raised, axis=-1, keepdims=True))
        probs = convert_to_half(raised / total).astype(jnp.float32)
        mixed_heads = jnp.einsum('hgqk,khd->qhgd', probs, value_float)
        return (convert_to_half(mixed_heads.reshape(rows_per_block, QUERY_HEADS * HEAD_SIZE)), highest[..., 0] + jnp.log(total[..., 0]))
    mixed_heads, log_total = lax.map(one_block, jnp.arange(count_of_rows // rows_per_block, dtype=jnp.int32))
    return (mixed_heads.reshape(count_of_rows, QUERY_HEADS * HEAD_SIZE), log_total)

def attend_back(query_rows, heads_of_keys, heads_of_values, mixed_heads, log_total, mixed_gradient, positions):
    count_of_rows = query_rows.shape[0]
    rows_per_block = min(QUERY_BLOCK, count_of_rows)
    query_groups = QUERY_HEADS // KEY_HEADS
    key_float = heads_of_keys.astype(jnp.float32)
    value_float = heads_of_values.astype(jnp.float32)
    scale = 1.0 / math.sqrt(HEAD_SIZE)

    def one_block(carry, block_index):
        grad_key_sum, grad_value_sum = carry
        start_offset = block_index * rows_per_block
        block_of_queries = lax.dynamic_slice_in_dim(query_rows, start_offset, rows_per_block, 0).astype(jnp.float32).reshape(rows_per_block, KEY_HEADS, query_groups, HEAD_SIZE)
        block_gradient = lax.dynamic_slice_in_dim(mixed_gradient, start_offset, rows_per_block, 0).astype(jnp.float32).reshape(rows_per_block, KEY_HEADS, query_groups, HEAD_SIZE)
        output_block = lax.dynamic_slice_in_dim(mixed_heads, start_offset, rows_per_block, 0).astype(jnp.float32).reshape(rows_per_block, KEY_HEADS, query_groups, HEAD_SIZE)
        current = lax.dynamic_slice_in_dim(positions, start_offset, rows_per_block, 0)
        visible = positions[None, :] <= current[:, None]
        delta = jnp.transpose(lax.optimization_barrier(jnp.sum(block_gradient * output_block, axis=-1)), (1, 2, 0))
        scores = jnp.einsum('qhgd,khd->hgqk', block_of_queries, key_float) * scale
        probs = jnp.where(visible[None, None], jnp.exp(scores - log_total[block_index][..., None]), 0.0)
        grad_probs = jnp.einsum('qhgd,khd->hgqk', block_gradient, value_float)
        grad_scores = convert_to_half(probs * (grad_probs - delta[..., None])).astype(jnp.float32)
        probs_half = convert_to_half(probs).astype(jnp.float32)
        grad_value_sum = grad_value_sum + jnp.einsum('hgqk,qhgd->khd', probs_half, block_gradient)
        grad_key_sum = grad_key_sum + jnp.einsum('hgqk,qhgd->khd', grad_scores, block_of_queries) * scale
        grad_query = jnp.einsum('hgqk,khd->qhgd', grad_scores, key_float) * scale
        return ((grad_key_sum, grad_value_sum), grad_query.reshape(rows_per_block, QUERY_HEADS * HEAD_SIZE))
    zero_filled = jnp.zeros((count_of_rows, KEY_HEADS, HEAD_SIZE), jnp.float32)
    sums, grad_queries = lax.scan(one_block, (zero_filled, zero_filled), jnp.arange(count_of_rows // rows_per_block, dtype=jnp.int32))
    return (grad_queries.reshape(count_of_rows, QUERY_HEADS * HEAD_SIZE), sums[0], sums[1])

def layer_forward(hidden, weights, cosine_values, sine_values, positions):
    w_query, key_projection, value_projection, w_output, w_gate, w_up, w_down, gain_first, gain_second = weights
    count_of_rows = hidden.shape[0]
    normed_first, factor_first, attention_input = norm_forward(hidden, gain_first)
    query_rows = convert_to_half(apply_rotation(matrix_product(attention_input, w_query).reshape(count_of_rows, QUERY_HEADS, HEAD_SIZE), cosine_values, sine_values))
    heads_of_keys = convert_to_half(apply_rotation(matrix_product(attention_input, key_projection).reshape(count_of_rows, KEY_HEADS, HEAD_SIZE), cosine_values, sine_values))
    heads_of_values = convert_to_half(matrix_product(attention_input, value_projection)).reshape(count_of_rows, KEY_HEADS, HEAD_SIZE)
    mixed_heads, log_total = attend(query_rows.reshape(count_of_rows, QUERY_HEADS * HEAD_SIZE), heads_of_keys, heads_of_values, positions)
    middle = hidden + matrix_product(mixed_heads, w_output)
    normed_second, factor_second, feed_input = norm_forward(middle, gain_second)
    gate_values = matrix_product(feed_input, w_gate)
    up_values = matrix_product(feed_input, w_up)
    hidden_units = convert_to_half(jax.nn.silu(gate_values) * up_values)
    result = middle + matrix_product(hidden_units, w_down)
    saved = (normed_first, factor_first, attention_input, query_rows.reshape(count_of_rows, QUERY_HEADS * HEAD_SIZE), heads_of_keys, heads_of_values, mixed_heads, log_total, normed_second, factor_second, feed_input, gate_values, up_values, hidden_units)
    return (result, saved)

def layer_backward(hidden, weights, cosine_values, sine_values, positions, carried):
    w_query, key_projection, value_projection, w_output, w_gate, w_up, w_down, gain_first, gain_second = weights
    count_of_rows = hidden.shape[0]
    result, saved = layer_forward(hidden, weights, cosine_values, sine_values, positions)
    normed_first, factor_first, attention_input, query_rows, heads_of_keys, heads_of_values, mixed_heads, log_total, normed_second, factor_second, feed_input, gate_values, up_values, hidden_units = saved
    grad_feed = convert_to_half(carried)
    down_grad = matrix_product(hidden_units.T, grad_feed)
    grad_units = matrix_product(grad_feed, w_down.T)
    sigmoid_gate = jax.nn.sigmoid(gate_values)
    grad_up = convert_to_half(grad_units * gate_values * sigmoid_gate)
    grad_gate = convert_to_half(grad_units * up_values * sigmoid_gate * (1.0 + gate_values * (1.0 - sigmoid_gate)))
    gate_grad = matrix_product(feed_input.T, grad_gate)
    up_grad = matrix_product(feed_input.T, grad_up)
    grad_feed_in = matrix_product(grad_gate, w_gate.T) + matrix_product(grad_up, w_up.T)
    grad_norm_second, gain_second_grad = norm_backward(grad_feed_in, normed_second, factor_second, gain_second)
    grad_middle = carried + grad_norm_second
    grad_mixed_in = convert_to_half(grad_middle)
    output_grad = matrix_product(mixed_heads.T, grad_mixed_in)
    mixed_gradient = convert_to_half(matrix_product(grad_mixed_in, w_output.T))
    grad_queries, key_gradients, value_gradients = attend_back(query_rows, heads_of_keys, heads_of_values, mixed_heads, log_total, mixed_gradient, positions)
    grad_query_in = convert_to_half(inverse_rotation(grad_queries.reshape(count_of_rows, QUERY_HEADS, HEAD_SIZE), cosine_values, sine_values).reshape(count_of_rows, QUERY_HEADS * HEAD_SIZE))
    incoming_key_gradient = convert_to_half(inverse_rotation(key_gradients, cosine_values, sine_values).reshape(count_of_rows, KEY_HEADS * HEAD_SIZE))
    incoming_value_gradient = convert_to_half(value_gradients.reshape(count_of_rows, KEY_HEADS * HEAD_SIZE))
    query_grad = matrix_product(attention_input.T, grad_query_in)
    key_grad = matrix_product(attention_input.T, incoming_key_gradient)
    value_grad = matrix_product(attention_input.T, incoming_value_gradient)
    grad_attend = matrix_product(grad_query_in, w_query.T) + matrix_product(incoming_key_gradient, key_projection.T) + matrix_product(incoming_value_gradient, value_projection.T)
    grad_norm_first, gain_first_grad = norm_backward(grad_attend, normed_first, factor_first, gain_first)
    return (grad_middle + grad_norm_first, (query_grad, key_grad, value_grad, output_grad, gate_grad, up_grad, down_grad, gain_first_grad, gain_second_grad))

def reference(block_input, pair_of_device, query_weight, key_weight, value_matrix, output_weight, gate_weight, up_weight, down_weight, attention_gain, feedforward_gain, output_cotangent):
    positions = key_positions(pair_of_device)
    cosine_values, sine_values = rope_tables(positions)

    def layer_weights(layer_index):
        return (query_weight[layer_index], key_weight[layer_index], value_matrix[layer_index], output_weight[layer_index], gate_weight[layer_index], up_weight[layer_index], down_weight[layer_index], attention_gain[layer_index], feedforward_gain[layer_index])

    def one_sequence(operands):
        hidden, carried = operands
        layer_inputs = []
        for layer_index in range(DECODER_LAYERS):
            layer_inputs.append(hidden)
            hidden, unused_saved = layer_forward(hidden, layer_weights(layer_index), cosine_values, sine_values, positions)
        layer_grads = [None] * DECODER_LAYERS
        for layer_index in reversed(range(DECODER_LAYERS)):
            carried, layer_grads[layer_index] = layer_backward(layer_inputs[layer_index], layer_weights(layer_index), cosine_values, sine_values, positions, carried)
        stacked = tuple((jnp.stack([layer_grads[layer_index][member_index] for layer_index in range(DECODER_LAYERS)]) for member_index in range(9)))
        return (hidden, carried, stacked)
    outputs, input_grad, stacked = lax.map(one_sequence, (block_input, output_cotangent))
    totals = [lax.optimization_barrier(jnp.sum(member, axis=0)) for member in stacked]
    return (outputs, input_grad, totals[0], totals[1], totals[2], totals[3], totals[4], totals[5], totals[6], totals[7], totals[8])
```

```python
import math

import jax
import jax.numpy as jnp
from jax import lax
from jax.experimental import pallas as pl
from jax.experimental.pallas import tpu as pltpu
from jax.sharding import PartitionSpec as P

QUERY_HEADS = 15
KEY_HEADS = 5
HEAD_SIZE = 64
GROUP = QUERY_HEADS // KEY_HEADS
QUERY_WIDTH = QUERY_HEADS * HEAD_SIZE
KEY_WIDTH = KEY_HEADS * HEAD_SIZE
EPSILON = 1e-05
THETA = 100000.0
SCALE = 1.0 / math.sqrt(HEAD_SIZE)
F32 = jnp.float32
BF16 = jnp.bfloat16


def dot_nn(left, right):
    return lax.dot_general(left, right, (((1,), (0,)), ((), ())), preferred_element_type=F32)


def dot_nt(left, right):
    return lax.dot_general(left, right, (((1,), (1,)), ((), ())), preferred_element_type=F32)


def dot_tn(left, right):
    return lax.dot_general(left, right, (((0,), (0,)), ((), ())), preferred_element_type=F32)


def swap(value, axis, bit):
    size = lax.axis_size(axis)
    return lax.ppermute(value, axis, [(i, i ^ bit) for i in range(size)])


def bits_of(axis):
    size = lax.axis_size(axis)
    result = []
    bit = 1
    while bit < size:
        result.append(bit)
        bit *= 2
    return result


def gather_blocks(value, axis):
    blocks = {0: value}
    order = [0]
    for bit in reversed(bits_of(axis)):
        for j in list(order):
            blocks[j ^ bit] = swap(blocks[j], axis, bit)
            order.append(j ^ bit)
    return [blocks[j] for j in range(len(order))]


def scatter_blocks(blocks, axis):
    blocks = list(blocks)
    count = len(blocks)
    bits = bits_of(axis)
    for bit in bits:
        last = bit == bits[-1]
        for j in reversed(range(0, count, 2 * bit)):
            received = swap(blocks[j + bit], axis, bit)
            total = blocks[j].astype(F32) + received.astype(F32)
            blocks[j] = total if last else total.astype(BF16)
    return blocks[0]


def exchange_blocks(blocks, axis):
    return [blocks[0]] + [swap(blocks[j], axis, j) for j in range(1, len(blocks))]


def reduce_over_ctx(value):
    own = lax.axis_index("ctx")
    bits = bits_of("ctx")
    for k, bit in enumerate(bits):
        lead, count, rows, width = value.shape
        pairs = value.reshape(lead, count // 2, 2, rows, width)
        side = (own >> k) & 1
        kept = lax.dynamic_index_in_dim(pairs, side, 2, keepdims=False)
        sent = lax.dynamic_index_in_dim(pairs, 1 - side, 2, keepdims=False)
        total = kept.astype(F32) + swap(sent, "ctx", bit).astype(F32)
        value = total if bit == bits[-1] else total.astype(BF16)
    return value[:, 0]


def sum_everywhere(value):
    for axis in ("fsdp", "ctx"):
        for bit in bits_of(axis):
            value = value + swap(value, axis, bit)
    return value


def launch(body, outs, scalars, arrays, scratch=()):
    in_specs = [pl.BlockSpec(memory_space=pltpu.SMEM) for _ in scalars]
    in_specs += [pl.BlockSpec(memory_space=pltpu.VMEM) for _ in arrays]
    return pl.pallas_call(
        body,
        out_shape=[jax.ShapeDtypeStruct(shape, dtype) for shape, dtype in outs],
        in_specs=in_specs,
        out_specs=[pl.BlockSpec(memory_space=pltpu.VMEM) for _ in outs],
        scratch_shapes=list(scratch),
        compiler_params=pltpu.CompilerParams(vmem_limit_bytes=60 * 1024 * 1024),
    )(*scalars, *arrays)


def rotated(values, cosine, sine):
    width = values.shape[-1]
    lane = lax.broadcasted_iota(jnp.int32, values.shape, 1)
    ahead = pltpu.roll(values, width - HEAD_SIZE // 2, 1)
    behind = pltpu.roll(values, HEAD_SIZE // 2, 1)
    other = jnp.where((lane % HEAD_SIZE) < HEAD_SIZE // 2, ahead, behind)
    repeat = width // cosine.shape[-1]
    return values * jnp.tile(cosine, (1, repeat)) + other * jnp.tile(sine, (1, repeat))


def norm_of(hidden):
    factor = lax.rsqrt(jnp.mean(hidden * hidden, axis=-1, keepdims=True) + EPSILON)
    return hidden * factor, factor


def prepare_body(parts):
    def body(hidden_ref, cotangent_ref, gain_ref, input_ref, feed_ref):
        normed, _ = norm_of(hidden_ref[...])
        attend = (normed * gain_ref[...]).astype(BF16)
        feed = cotangent_ref[...].astype(BF16)
        wide = attend.shape[-1] // parts
        for b in range(parts):
            input_ref[b] = attend[:, b * wide : (b + 1) * wide]
            feed_ref[b] = feed[:, b * wide : (b + 1) * wide]

    return body


def project_body(parts):
    def body(*refs):
        own = refs[0][0]
        input_ref, cosine_ref, sine_ref = refs[1:4]
        weights = refs[4 : 4 + 3 * parts]
        query_ref, pair_ref = refs[4 + 3 * parts :]
        query = key = value = None
        for j in range(parts):
            rows = input_ref[own ^ j]
            terms = [dot_nn(rows, weights[m * parts + j][...]) for m in range(3)]
            if query is None:
                query, key, value = terms
            else:
                query, key, value = query + terms[0], key + terms[1], value + terms[2]
        both = jnp.concatenate([query, key], axis=1)
        both = rotated(both, cosine_ref[...], sine_ref[...]).astype(BF16)
        query_ref[...] = both[:, :QUERY_WIDTH]
        pair_ref[:, :KEY_WIDTH] = both[:, QUERY_WIDTH:]
        pair_ref[:, KEY_WIDTH:] = value.astype(BF16)

    return body


def stack_group(values, head, half):
    pieces = []
    for start in (half, 0):
        for g in range(GROUP):
            lane = (head * GROUP + g) * HEAD_SIZE
            pieces.append(values[start : start + half, lane : lane + HEAD_SIZE])
    return jnp.concatenate(pieces, axis=0)


def unstack_groups(groups, half):
    late = [g[i * half : (i + 1) * half] for g in groups for i in range(GROUP)]
    early = [g[(GROUP + i) * half : (GROUP + i + 1) * half] for g in groups for i in range(GROUP)]
    return jnp.concatenate(
        [jnp.concatenate(early, axis=1), jnp.concatenate(late, axis=1)], axis=0
    )


def split_keys(pair_refs, early_scratch, late_scratch, half):
    for j, pair_ref in enumerate(pair_refs):
        early_scratch[j * half : (j + 1) * half, :] = pair_ref[:half, :]
        late_scratch[j * half : (j + 1) * half, :] = pair_ref[half:, :]


def attend_body(parts, count, half):
    wide = GROUP * half

    def body(*refs):
        own = refs[0][0]
        query_ref, early_pos, late_pos, row_pos, hidden_ref, gain_ref = refs[1:7]
        pair_refs = refs[7 : 7 + count]
        output_refs = refs[7 + count : 7 + count + parts]
        mixed_ref, total_ref, middle_ref, feed_ref = refs[7 + count + parts : 11 + count + parts]
        early_scratch, late_scratch, block_scratch = refs[11 + count + parts :]
        split_keys(pair_refs, early_scratch, late_scratch, half)
        query = query_ref[...] * SCALE
        visible_early = early_pos[...] <= row_pos[...]
        visible_late = late_pos[...] <= row_pos[:, :wide]
        groups = []
        for h in range(KEY_HEADS):
            lane = h * HEAD_SIZE
            rows = stack_group(query, h, half)
            key_early = early_scratch[:, lane : lane + HEAD_SIZE]
            key_late = late_scratch[:, lane : lane + HEAD_SIZE]
            value_early = early_scratch[:, KEY_WIDTH + lane : KEY_WIDTH + lane + HEAD_SIZE]
            value_late = late_scratch[:, KEY_WIDTH + lane : KEY_WIDTH + lane + HEAD_SIZE]
            score_early = jnp.where(visible_early, dot_nt(key_early, rows), -1e30)
            score_late = jnp.where(visible_late, dot_nt(key_late, rows[:wide]), -1e30)
            high_early = jnp.max(score_early, axis=0, keepdims=True)
            high_late = jnp.max(score_late, axis=0, keepdims=True)
            high_late = jnp.maximum(high_early[:, :wide], high_late)
            high = jnp.concatenate([high_late, high_early[:, wide:]], axis=1)
            raised_early = jnp.exp(score_early - high)
            raised_late = jnp.exp(score_late - high_late)
            sum_early = jnp.sum(raised_early, axis=0, keepdims=True)
            sum_late = sum_early[:, :wide] + jnp.sum(raised_late, axis=0, keepdims=True)
            total = jnp.concatenate([sum_late, sum_early[:, wide:]], axis=1)
            inverse = 1.0 / total
            mixed_early = dot_tn(value_early, (raised_early * inverse).astype(BF16))
            mixed_late = dot_tn(value_late, (raised_late * inverse[:, :wide]).astype(BF16))
            joined = jnp.concatenate(
                [mixed_early[:, :wide] + mixed_late, mixed_early[:, wide:]], axis=1
            )
            groups.append(joined.T)
            total_ref[h : h + 1, :] = high + jnp.log(total)
        mixed = unstack_groups(groups, half).astype(BF16)
        mixed_ref[...] = mixed
        for j in range(parts):
            block_scratch[own ^ j] = dot_nn(mixed, output_refs[j][...])
        middle = hidden_ref[...] + jnp.concatenate(
            [block_scratch[b] for b in range(parts)], axis=1
        )
        middle_ref[...] = middle
        normed, _ = norm_of(middle)
        feed = (normed * gain_ref[...]).astype(BF16)
        block = feed.shape[-1] // parts
        for b in range(parts):
            feed_ref[b] = feed[:, b * block : (b + 1) * block]

    return body


def feed_body(parts):
    def body(*refs):
        own = refs[0][0]
        input_refs = refs[1 : 1 + parts]
        feed_refs = refs[1 + parts : 1 + 2 * parts]
        weight_refs = refs[1 + 2 * parts : 1 + 3 * parts]
        back_refs = refs[1 + 3 * parts : 1 + 4 * parts]
        hidden_ref, gate_ref, up_ref = refs[1 + 4 * parts :]
        rows = input_refs[0].shape[1]

        def gathered(block_refs, b):
            return jnp.concatenate([r[b] for r in block_refs], axis=0)

        gate = up = units = None
        for j in range(parts):
            block = gathered(input_refs, own ^ j)
            feed = gathered(feed_refs, own ^ j)
            terms = [
                dot_nt(block, weight_refs[j][0]),
                dot_nt(block, weight_refs[j][1]),
                dot_nt(feed, weight_refs[j][2]),
            ]
            if gate is None:
                gate, up, units = terms
            else:
                gate, up, units = gate + terms[0], up + terms[1], units + terms[2]
        sigmoid = 1.0 / (1.0 + jnp.exp(-gate))
        silu = gate * sigmoid
        hidden_ref[...] = (silu * up).astype(BF16)
        grad_up = (units * silu).astype(BF16)
        grad_gate = (units * up * sigmoid * (1.0 + gate * (1.0 - sigmoid))).astype(BF16)
        gate_ref[...] = grad_gate
        up_ref[...] = grad_up
        for j in range(parts):
            back = dot_nn(grad_gate, weight_refs[j][0]) + dot_nn(grad_up, weight_refs[j][1])
            back = back.astype(BF16)
            for i in range(parts):
                back_refs[i][own ^ j] = back[i * rows : (i + 1) * rows]

    return body


def feed_grads_body(parts):
    def body(*refs):
        own = refs[0][0]
        input_refs = refs[1 : 1 + parts]
        feed_refs = refs[1 + parts : 1 + 2 * parts]
        weight_refs = refs[1 + 2 * parts : 1 + 3 * parts]
        hidden_ref, gate_ref, up_ref = refs[1 + 3 * parts : 4 + 3 * parts]
        grad_refs = refs[4 + 3 * parts : 7 + 3 * parts]
        out_refs = refs[7 + 3 * parts :]
        rows = input_refs[0].shape[1]

        def gathered(block_refs, b):
            return jnp.concatenate([r[b] for r in block_refs], axis=0)

        for j in range(parts):
            block = gathered(input_refs, own ^ j)
            feed = gathered(feed_refs, own ^ j)
            grad_refs[0][j] = dot_tn(gate_ref[...], block).astype(BF16)
            grad_refs[1][j] = dot_tn(up_ref[...], block).astype(BF16)
            grad_refs[2][j] = dot_tn(hidden_ref[...], feed).astype(BF16)
        for j in range(parts):
            out = dot_nn(hidden_ref[...], weight_refs[j][2]).astype(BF16)
            for i in range(parts):
                out_refs[i][own ^ j] = out[i * rows : (i + 1) * rows]

    return body


def back_body(parts, count, half):
    wide = GROUP * half

    def body(*refs):
        own = refs[0][0]
        (
            back_ref,
            middle_ref,
            gain_ref,
            cotangent_ref,
            mixed_ref,
            query_ref,
            total_ref,
            early_pos,
            late_pos,
            row_pos,
            cosine_ref,
            sine_ref,
        ) = refs[1:13]
        pair_refs = refs[13 : 13 + count]
        output_refs = refs[13 + count : 13 + count + parts]
        at = 13 + count + parts
        grad_middle_ref, mixed_in_ref, gain_grad_ref, grad_query_ref = refs[at : at + 4]
        grad_pair_refs = refs[at + 4 : at + 4 + count]
        early_scratch, late_scratch = refs[at + 4 + count :]
        split_keys(pair_refs, early_scratch, late_scratch, half)
        normed, factor = norm_of(middle_ref[...])
        grad = jnp.concatenate([back_ref[b] for b in range(parts)], axis=1)
        gain_grad_ref[...] = jnp.sum(grad * normed, axis=0, keepdims=True)
        scaled = grad * gain_ref[...]
        grad_middle = cotangent_ref[...] + factor * (
            scaled - normed * jnp.mean(scaled * normed, axis=-1, keepdims=True)
        )
        grad_middle_ref[...] = grad_middle
        mixed_in = grad_middle.astype(BF16)
        block = mixed_in.shape[-1] // parts
        for b in range(parts):
            mixed_in_ref[b] = mixed_in[:, b * block : (b + 1) * block]
        mixed_grad = None
        for j in range(parts):
            term = dot_nt(mixed_in_ref[own ^ j], output_refs[j][...])
            mixed_grad = term if mixed_grad is None else mixed_grad + term
        mixed_grad = mixed_grad.astype(BF16)
        product = mixed_grad.astype(F32) * mixed_ref[...].astype(F32)
        query = query_ref[...] * SCALE
        visible_early = early_pos[...] <= row_pos[...]
        visible_late = late_pos[...] <= row_pos[:, :wide]
        groups = []
        grads_early = [[], []]
        grads_late = [[], []]
        for h in range(KEY_HEADS):
            lane = h * HEAD_SIZE
            rows = stack_group(query, h, half)
            outer = stack_group(mixed_grad, h, half)
            delta = jnp.sum(stack_group(product, h, half).T, axis=0, keepdims=True)
            log_total = total_ref[h : h + 1, :]
            key_early = early_scratch[:, lane : lane + HEAD_SIZE]
            key_late = late_scratch[:, lane : lane + HEAD_SIZE]
            value_early = early_scratch[:, KEY_WIDTH + lane : KEY_WIDTH + lane + HEAD_SIZE]
            value_late = late_scratch[:, KEY_WIDTH + lane : KEY_WIDTH + lane + HEAD_SIZE]
            probs = jnp.where(visible_early, jnp.exp(dot_nt(key_early, rows) - log_total), 0.0)
            score_grad = (probs * (dot_nt(value_early, outer) - delta)).astype(BF16)
            grads_early[1].append(dot_nn(probs.astype(BF16), outer))
            grads_early[0].append(dot_nn(score_grad, rows))
            query_early = dot_tn(key_early, score_grad)
            probs = jnp.where(
                visible_late, jnp.exp(dot_nt(key_late, rows[:wide]) - log_total[:, :wide]), 0.0
            )
            score_grad = (probs * (dot_nt(value_late, outer[:wide]) - delta[:, :wide])).astype(BF16)
            grads_late[1].append(dot_nn(probs.astype(BF16), outer[:wide]))
            grads_late[0].append(dot_nn(score_grad, rows[:wide]))
            query_late = dot_tn(key_late, score_grad)
            joined = jnp.concatenate(
                [query_early[:, :wide] + query_late, query_early[:, wide:]], axis=1
            )
            groups.append(joined.T)
        grad_query = unstack_groups(groups, half) * SCALE
        padded = jnp.concatenate([grad_query, jnp.zeros_like(grad_query[:, :HEAD_SIZE])], axis=1)
        padded = rotated(padded, cosine_ref[...], -sine_ref[...]).astype(BF16)
        grad_query_ref[...] = padded[:, :QUERY_WIDTH]
        pair_early = jnp.concatenate(grads_early[0] + grads_early[1], axis=1).astype(BF16)
        pair_late = jnp.concatenate(grads_late[0] + grads_late[1], axis=1).astype(BF16)
        for j in range(count):
            grad_pair_refs[j][:half, :] = pair_early[j * half : (j + 1) * half]
            grad_pair_refs[j][half:, :] = pair_late[j * half : (j + 1) * half]

    return body


def attention_grads_body(parts):
    def body(*refs):
        query_refs = refs[:parts]
        input_refs = refs[parts : 2 * parts]
        mixed_refs = refs[2 * parts : 3 * parts]
        mixed_in_refs = refs[3 * parts : 4 * parts]
        weight_refs = refs[4 * parts : 5 * parts]
        grad_ref, attend_ref = refs[5 * parts :]

        def rows_of(items):
            return jnp.concatenate([r[...] for r in items], axis=0)

        grad_ref[0] = dot_tn(rows_of(query_refs), rows_of(input_refs)).astype(BF16)
        grad_ref[1] = dot_tn(rows_of(mixed_refs), rows_of(mixed_in_refs)).astype(BF16)
        for j in range(parts):
            attend_ref[j] = dot_nt(query_refs[0][...], weight_refs[j][...])

    return body


def input_grad_body(parts):
    def body(*refs):
        own = refs[0][0]
        pair_grad_ref, cosine_ref, sine_ref, attend_ref, hidden_ref, gain_ref, middle_ref = refs[1:8]
        key_refs = refs[8 : 8 + parts]
        value_refs = refs[8 + parts : 8 + 2 * parts]
        pair_ref, grad_ref, gain_grad_ref, block_scratch = refs[8 + 2 * parts :]
        pair = pair_grad_ref[...]
        turned = rotated(pair, cosine_ref[...], -sine_ref[...])
        key = turned[:, :KEY_WIDTH].astype(BF16)
        value = pair[:, KEY_WIDTH:].astype(BF16)
        pair_ref[:, :KEY_WIDTH] = key
        pair_ref[:, KEY_WIDTH:] = value
        for j in range(parts):
            block_scratch[own ^ j] = (
                attend_ref[j] + dot_nt(key, key_refs[j][...]) + dot_nt(value, value_refs[j][...])
            )
        grad = jnp.concatenate([block_scratch[b] for b in range(parts)], axis=1)
        normed, factor = norm_of(hidden_ref[...])
        gain_grad_ref[...] = jnp.sum(grad * normed, axis=0, keepdims=True)
        scaled = grad * gain_ref[...]
        grad_ref[...] = middle_ref[...] + factor * (
            scaled - normed * jnp.mean(scaled * normed, axis=-1, keepdims=True)
        )

    return body


def pair_grads_body(parts):
    def body(*refs):
        pair_refs = refs[:parts]
        input_refs = refs[parts : 2 * parts]
        grad_ref = refs[2 * parts]

        def rows_of(items):
            return jnp.concatenate([r[...] for r in items], axis=0)

        grad_ref[...] = dot_tn(rows_of(pair_refs), rows_of(input_refs)).astype(BF16)

    return body


def shards(
    block_input,
    pair_of_device,
    query_weight,
    key_weight,
    value_matrix,
    output_weight,
    gate_weight,
    up_weight,
    down_weight,
    attention_gain,
    feedforward_gain,
    output_cotangent,
):
    hidden = block_input[0]
    cotangent = output_cotangent[0]
    rows, width = hidden.shape
    half = rows // 2
    count = lax.axis_size("ctx")
    parts = lax.axis_size("fsdp")
    own_ctx = lax.axis_index("ctx")
    own = lax.axis_index("fsdp")
    block = width // parts
    units = down_weight.shape[1]
    share = units // (count * parts)
    own_scalar = own.astype(jnp.int32).reshape(1)

    device_ids = jnp.arange(count, dtype=jnp.int32)
    relative = own_ctx.astype(jnp.int32) ^ device_ids
    pairs = jnp.sum(
        jnp.where(relative[:, None] == device_ids[None, :], pair_of_device[None, :], 0), axis=1
    )
    within = jnp.arange(half, dtype=jnp.int32)
    early_pos = (pairs[:, None] * half + within[None, :]).reshape(-1, 1)
    late_pos = ((2 * count - 1 - pairs)[:, None] * half + within[None, :]).reshape(-1, 1)
    own_early = pairs[0] * half + within
    own_late = (2 * count - 1 - pairs[0]) * half + within
    row_pos = jnp.concatenate([own_late] * GROUP + [own_early] * GROUP)[None, :]
    half_head = HEAD_SIZE // 2
    frequency = jnp.exp(
        jnp.arange(half_head, dtype=F32) * (-2.0 * math.log(THETA) / HEAD_SIZE)
    )
    positions = jnp.concatenate([own_early, own_late])
    angles = positions.astype(F32)[:, None] * frequency[None, :]
    cosine, sine = jnp.cos(angles), jnp.sin(angles)
    cosine = jnp.concatenate([cosine] * 4, axis=1)
    sine = jnp.concatenate([-sine, sine] * 2, axis=1)

    query_blocks = gather_blocks(query_weight[0], "fsdp")
    key_blocks = gather_blocks(key_weight[0], "fsdp")
    value_blocks = gather_blocks(value_matrix[0], "fsdp")

    attend_input, grad_feed = launch(
        prepare_body(parts),
        [((parts, rows, block), BF16), ((parts, rows, block), BF16)],
        [],
        [hidden, cotangent, attention_gain],
    )
    query, key_value = launch(
        project_body(parts),
        [((rows, QUERY_WIDTH), BF16), ((rows, 2 * KEY_WIDTH), BF16)],
        [own_scalar],
        [attend_input, cosine, sine, *query_blocks, *key_blocks, *value_blocks],
    )
    key_values = gather_blocks(key_value, "ctx")
    output_blocks = gather_blocks(output_weight[0], "fsdp")

    dealt = jnp.stack([gate_weight[0].T, up_weight[0].T, down_weight[0]])
    dealt = dealt.reshape(3, count, parts, share, block)
    pieces = [
        lax.dynamic_index_in_dim(dealt, own ^ j, 2, keepdims=False).reshape(3, count * share, block)
        for j in range(parts)
    ]
    feed_weights = exchange_blocks(pieces, "fsdp")
    feeds = gather_blocks(grad_feed, "fsdp")
    inputs_own = exchange_blocks(
        [lax.dynamic_index_in_dim(attend_input, own ^ j, 0, keepdims=False) for j in range(parts)],
        "fsdp",
    )

    mixed, log_total, middle, feed_input = launch(
        attend_body(parts, count, half),
        [
            ((rows, QUERY_WIDTH), BF16),
            ((KEY_HEADS, 2 * GROUP * half), F32),
            ((rows, width), F32),
            ((parts, rows, block), BF16),
        ],
        [own_scalar],
        [query, early_pos, late_pos, row_pos, hidden, feedforward_gain, *key_values, *output_blocks],
        [
            pltpu.VMEM((count * half, 2 * KEY_WIDTH), BF16),
            pltpu.VMEM((count * half, 2 * KEY_WIDTH), BF16),
            pltpu.VMEM((parts, rows, block), F32),
        ],
    )
    feed_inputs = gather_blocks(feed_input, "fsdp")
    mixed_all = gather_blocks(mixed, "fsdp")

    results = launch(
        feed_body(parts),
        [((parts, rows, block), BF16)] * parts
        + [((parts * rows, count * share), BF16)] * 3,
        [own_scalar],
        [*feed_inputs, *feeds, *feed_weights],
    )
    backs = results[:parts]
    hidden_units, grad_gate, grad_up = results[parts:]
    back = scatter_blocks(backs, "fsdp")
    results = launch(
        feed_grads_body(parts),
        [((parts, count * share, block), BF16)] * 3 + [((parts, rows, block), BF16)] * parts,
        [own_scalar],
        [*feed_inputs, *feeds, *feed_weights, hidden_units, grad_gate, grad_up],
    )
    feed_grads = results[:3]
    outs = scatter_blocks(results[3:], "fsdp")
    block_output = middle + outs.transpose(1, 0, 2).reshape(rows, width)

    results = launch(
        back_body(parts, count, half),
        [
            ((rows, width), F32),
            ((parts, rows, block), BF16),
            ((1, width), F32),
            ((rows, QUERY_WIDTH), BF16),
        ]
        + [((rows, 2 * KEY_WIDTH), BF16)] * count,
        [own_scalar],
        [
            back,
            middle,
            feedforward_gain,
            cotangent,
            mixed,
            query,
            log_total,
            early_pos,
            late_pos,
            row_pos,
            cosine,
            sine,
            *key_values,
            *output_blocks,
        ],
        [
            pltpu.VMEM((count * half, 2 * KEY_WIDTH), BF16),
            pltpu.VMEM((count * half, 2 * KEY_WIDTH), BF16),
        ],
    )
    grad_middle, mixed_in, feed_gain_part, grad_query = results[:4]
    pair_grad = scatter_blocks(results[4:], "ctx")
    grad_queries = gather_blocks(grad_query, "fsdp")
    mixed_in_own = exchange_blocks(
        [lax.dynamic_index_in_dim(mixed_in, own ^ j, 0, keepdims=False) for j in range(parts)],
        "fsdp",
    )
    query_output_grads, attend_part = launch(
        attention_grads_body(parts),
        [((2, QUERY_WIDTH, block), BF16), ((parts, rows, block), F32)],
        [],
        [*grad_queries, *inputs_own, *mixed_all, *mixed_in_own, *query_blocks],
    )
    pair_in, input_grad, attention_gain_part = launch(
        input_grad_body(parts),
        [((rows, 2 * KEY_WIDTH), BF16), ((rows, width), F32), ((1, width), F32)],
        [own_scalar],
        [
            pair_grad,
            cosine,
            sine,
            attend_part,
            hidden,
            attention_gain,
            grad_middle,
            *key_blocks,
            *value_blocks,
        ],
        [pltpu.VMEM((parts, rows, block), F32)],
    )
    pair_all = gather_blocks(pair_in, "fsdp")
    (key_value_grads,) = launch(
        pair_grads_body(parts),
        [((2 * KEY_WIDTH, block), BF16)],
        [],
        [*pair_all, *inputs_own],
    )

    feed_reduced = [
        reduce_over_ctx(g.reshape(parts, count, share, block)).astype(BF16) for g in feed_grads
    ]
    query_output = reduce_over_ctx(query_output_grads.reshape(2, count, QUERY_WIDTH // count, block))
    key_value_own = reduce_over_ctx(key_value_grads.reshape(2, count, KEY_WIDTH // count, block))
    stacked = jnp.stack(feed_reduced, axis=1)
    received = exchange_blocks([stacked[j] for j in range(parts)], "fsdp")
    received = jnp.stack(received)
    ordered = jnp.concatenate(
        [lax.dynamic_index_in_dim(received, own ^ b, 0, keepdims=False) for b in range(parts)],
        axis=1,
    ).astype(F32)

    attention_sums = sum_everywhere(attention_gain_part)
    feed_sums = sum_everywhere(feed_gain_part)
    return (
        block_output[None],
        input_grad[None],
        query_output[0].T[None],
        key_value_own[0].T[None],
        key_value_own[1].T[None],
        query_output[1][None],
        ordered[0].T[None],
        ordered[1].T[None],
        ordered[2][None],
        attention_sums,
        feed_sums,
    )


def solution(mesh):
    return jax.shard_map(
        shards,
        mesh=mesh,
        in_specs=(
            P("fsdp", "ctx", None),
            P(),
            P(None, "fsdp", None),
            P(None, "fsdp", None),
            P(None, "fsdp", None),
            P(None, None, "fsdp"),
            P(None, "fsdp", None),
            P(None, "fsdp", None),
            P(None, None, "fsdp"),
            P(),
            P(),
            P("fsdp", "ctx", None),
        ),
        out_specs=(
            P("fsdp", "ctx", None),
            P("fsdp", "ctx", None),
            P(None, "fsdp", "ctx"),
            P(None, "fsdp", "ctx"),
            P(None, "fsdp", "ctx"),
            P(None, "ctx", "fsdp"),
            P(None, "fsdp", "ctx"),
            P(None, "fsdp", "ctx"),
            P(None, "ctx", "fsdp"),
            P(),
            P(),
        ),
        check_vma=False,
    )
```

```python
import math

import jax
import jax.numpy as jnp
from jax import lax
from jax.experimental import pallas as pl
from jax.experimental.pallas import tpu as pltpu
from jax.sharding import PartitionSpec as P

QUERY_HEADS = 15
KEY_HEADS = 5
HEAD_SIZE = 64
GROUP = QUERY_HEADS // KEY_HEADS
QUERY_WIDTH = QUERY_HEADS * HEAD_SIZE
KEY_WIDTH = KEY_HEADS * HEAD_SIZE
EPSILON = 1e-05
THETA = 100000.0
SCALE = 1.0 / math.sqrt(HEAD_SIZE)
F32 = jnp.float32
BF16 = jnp.bfloat16


def dot_nn(left, right):
    return lax.dot_general(left, right, (((1,), (0,)), ((), ())), preferred_element_type=F32)


def dot_nt(left, right):
    return lax.dot_general(left, right, (((1,), (1,)), ((), ())), preferred_element_type=F32)


def dot_tn(left, right):
    return lax.dot_general(left, right, (((0,), (0,)), ((), ())), preferred_element_type=F32)


def swap(value, axis, bit):
    size = lax.axis_size(axis)
    return lax.ppermute(value, axis, [(i, i ^ bit) for i in range(size)])


def bits_of(axis):
    size = lax.axis_size(axis)
    result = []
    bit = 1
    while bit < size:
        result.append(bit)
        bit *= 2
    return result


def gather_blocks(value, axis):
    blocks = {0: value}
    order = [0]
    for bit in reversed(bits_of(axis)):
        for j in list(order):
            blocks[j ^ bit] = swap(blocks[j], axis, bit)
            order.append(j ^ bit)
    return [blocks[j] for j in range(len(order))]


def gather_levels(value, axis, beside):
    count = lax.axis_size(axis)
    blocks = {0: value}
    level = [0]
    extras = []
    while len(blocks) < count:
        width = bin(level[0]).count("1") + 1
        token = blocks[level[-1]]
        level = [j for j in range(count) if bin(j).count("1") == width]
        for j in sorted(level, reverse=True):
            blocks[j] = swap(blocks[j & (j - 1)], axis, j & -j)
        extra = beside[width - 1](token) if width <= len(beside) else ()
        gated, extra = lax.optimization_barrier((tuple(blocks[j] for j in level), extra))
        blocks.update(zip(level, gated))
        extras.append(extra)
    return [blocks[j] for j in range(count)], extras


def exchange_blocks(blocks, axis):
    return [blocks[0]] + [swap(blocks[j], axis, j) for j in range(1, len(blocks))]


def split_side(value, own, k):
    pairs = value.reshape(value.shape[0] // 2, 2, *value.shape[1:])
    side = (own >> k) & 1
    kept = lax.dynamic_index_in_dim(pairs, side, 1, keepdims=False)
    return kept, lax.dynamic_index_in_dim(pairs, 1 - side, 1, keepdims=False)


def half_step(kept, received):
    total = (kept.astype(F32) + received.astype(F32)).astype(BF16)
    pairs = total.reshape(total.shape[0] // 2, 2, *total.shape[1:])
    return pairs[:, 0], pairs[:, 1]


class Hbm:
    def __init__(self, value, index=()):
        self.value, self.index = value, index


def hbm(values):
    return [Hbm(v) for v in values]


class LateInput:
    def __init__(self, buffer, copy):
        self.buffer, self.copy, self.waiting = buffer, copy, True

    def ready(self):
        if self.waiting:
            self.copy.wait()
            self.waiting = False

    @property
    def shape(self):
        return self.buffer.shape

    def __getitem__(self, index):
        self.ready()
        return self.buffer[index]


class LateOutput:
    def __init__(self, buffer, copy):
        self.buffer, self.copy, self.started = buffer, copy, False

    def flush(self):
        if not self.started:
            self.copy.start()
            self.started = True

    def __getitem__(self, index):
        return self.buffer[index]

    def __setitem__(self, index, value):
        self.buffer[index] = value


def launch(body, outs, scalars, arrays, scratch=()):
    late_in = [isinstance(a, Hbm) for a in arrays]
    values = [a.value if isinstance(a, Hbm) else a for a in arrays]
    picks = [a.index if isinstance(a, Hbm) else () for a in arrays]
    late_out = [len(o) == 3 for o in outs]
    count_in, count_out = sum(late_in), sum(late_out)
    vmem = pl.BlockSpec(memory_space=pltpu.VMEM)
    away = pl.BlockSpec(memory_space=pl.ANY)
    buffers = [
        pltpu.VMEM(v.shape[len(p) :], v.dtype) for v, p, late in zip(values, picks, late_in) if late
    ]
    buffers += [pltpu.VMEM(o[0], o[1]) for o, late in zip(outs, late_out) if late]
    if buffers:
        buffers.append(pltpu.SemaphoreType.DMA((count_in + count_out,)))

    def wrapped(*refs):
        at = len(scalars)
        items = list(refs[:at])
        ins = refs[at : at + len(values)]
        at += len(values)
        results = refs[at : at + len(outs)]
        at += len(outs)
        own_scratch = refs[at : at + len(scratch)]
        spare = list(refs[at + len(scratch) :])
        late_ins, late_outs = [], []
        slot = 0
        for ref, pick, late in zip(ins, picks, late_in):
            if late:
                source = ref.at[pick] if pick else ref
                copy = pltpu.make_async_copy(source, spare[slot], spare[-1].at[slot])
                copy.start()
                late_ins.append(LateInput(spare[slot], copy))
                items.append(late_ins[-1])
                slot += 1
            else:
                items.append(ref)
        for ref, late in zip(results, late_out):
            if late:
                copy = pltpu.make_async_copy(spare[slot], ref, spare[-1].at[slot])
                late_outs.append(LateOutput(spare[slot], copy))
                items.append(late_outs[-1])
                slot += 1
            else:
                items.append(ref)
        body(*items, *own_scratch)
        for item in late_ins:
            item.ready()
        for item in late_outs:
            item.flush()
        for item in late_outs:
            item.copy.wait()

    return pl.pallas_call(
        wrapped,
        out_shape=[jax.ShapeDtypeStruct(o[0], o[1]) for o in outs],
        in_specs=[pl.BlockSpec(memory_space=pltpu.SMEM) for _ in scalars]
        + [away if late else vmem for late in late_in],
        out_specs=[away if late else vmem for late in late_out],
        scratch_shapes=list(scratch) + buffers,
        compiler_params=pltpu.CompilerParams(vmem_limit_bytes=60 * 1024 * 1024),
    )(*scalars, *values)


def after(value, *others):
    return lax.optimization_barrier((value, *others))[0]


def rotated(values, cosine, sine):
    width = values.shape[-1]
    lane = lax.broadcasted_iota(jnp.int32, values.shape, 1)
    ahead = pltpu.roll(values, width - HEAD_SIZE // 2, 1)
    behind = pltpu.roll(values, HEAD_SIZE // 2, 1)
    other = jnp.where((lane % HEAD_SIZE) < HEAD_SIZE // 2, ahead, behind)
    repeat = width // cosine.shape[-1]
    return values * jnp.tile(cosine, (1, repeat)) + other * jnp.tile(sine, (1, repeat))


def norm_of(hidden):
    factor = lax.rsqrt(jnp.mean(hidden * hidden, axis=-1, keepdims=True) + EPSILON)
    return hidden * factor, factor


def prepare_body(parts):
    def body(*refs):
        hidden_ref, cotangent_ref, gain_ref, query_ref, key_ref, value_ref = refs[:6]
        weight_ref, input_ref, feed_ref, rows_ref = refs[6:]
        weight_ref[...] = jnp.concatenate(
            [query_ref[...], key_ref[...].T, value_ref[...].T], axis=1
        )
        weight_ref.flush()
        hidden = hidden_ref[...].T
        cotangent = cotangent_ref[...].T
        rows_ref[0] = hidden
        rows_ref[1] = cotangent
        normed, _ = norm_of(hidden)
        attend = (normed * gain_ref[...]).astype(BF16)
        feed = cotangent.astype(BF16)
        block = attend.shape[-1] // parts
        for b in range(parts):
            input_ref[b, :, :block] = attend[:, b * block : (b + 1) * block]
            feed_ref[b, :, :block] = feed[:, b * block : (b + 1) * block]

    return body


def deal_body(parts, count):
    def body(*refs):
        own = refs[0][0]
        weight_refs = refs[1:4]
        own_ref, near_ref, far_ref, scratch = refs[4:]
        for m in range(3):
            values = weight_refs[m][...]
            chunk = values.shape[1] // count
            share = chunk // parts
            for g in range(parts):
                scratch[g] = jnp.concatenate(
                    [
                        values[:, c * chunk + g * share : c * chunk + (g + 1) * share]
                        for c in range(count)
                    ],
                    axis=1,
                )
            far_ref[0, m] = scratch[own ^ 2]
            far_ref[1, m] = scratch[own ^ 3]
            own_ref[m] = scratch[own]
            near_ref[m] = scratch[own ^ 1]

    return body


def project_body(parts, block):
    def body(*refs):
        own = refs[0][0]
        input_ref, cosine_ref, sine_ref = refs[1:4]
        weight_refs = refs[4 : 4 + parts]
        query_ref, pair_ref = refs[4 + parts :]
        result = None
        for j in range(parts):
            term = dot_nn(input_ref[own ^ j][:, :block], weight_refs[j][...])
            result = term if result is None else result + term
        both = rotated(result[:, : QUERY_WIDTH + KEY_WIDTH], cosine_ref[...], sine_ref[...])
        both = both.astype(BF16)
        query_ref[...] = both[:, :QUERY_WIDTH]
        pair_ref[:, :KEY_WIDTH] = both[:, QUERY_WIDTH:]
        pair_ref[:, KEY_WIDTH:] = result[:, QUERY_WIDTH + KEY_WIDTH :].astype(BF16)

    return body


def stack_group(values, head, half):
    pieces = []
    for start in (half, 0):
        for g in range(GROUP):
            lane = (head * GROUP + g) * HEAD_SIZE
            pieces.append(values[start : start + half, lane : lane + HEAD_SIZE])
    return jnp.concatenate(pieces, axis=0)


def unstack_groups(groups, half):
    late = [g[i * half : (i + 1) * half] for g in groups for i in range(GROUP)]
    early = [g[(GROUP + i) * half : (GROUP + i + 1) * half] for g in groups for i in range(GROUP)]
    return jnp.concatenate(
        [jnp.concatenate(early, axis=1), jnp.concatenate(late, axis=1)], axis=0
    )


def split_keys(pair_refs, early_scratch, late_scratch, half):
    for j, pair_ref in enumerate(pair_refs):
        early_scratch[j * half : (j + 1) * half, :] = pair_ref[:half, :]
        late_scratch[j * half : (j + 1) * half, :] = pair_ref[half:, :]


def attend_body(parts, count, half):
    wide = GROUP * half

    def body(*refs):
        own = refs[0][0]
        query_ref, early_pos, late_pos, row_pos, rows_ref, gain_ref = refs[1:7]
        pair_refs = refs[7 : 7 + count]
        output_refs = refs[7 + count : 7 + count + parts]
        mixed_ref, total_ref, middle_ref, feed_ref = refs[7 + count + parts : 11 + count + parts]
        early_scratch, late_scratch, block_scratch = refs[11 + count + parts :]
        split_keys(pair_refs, early_scratch, late_scratch, half)
        query = query_ref[...] * SCALE
        visible_early = early_pos[...] <= row_pos[...]
        visible_late = late_pos[...] <= row_pos[:, :wide]
        groups = []
        for h in range(KEY_HEADS):
            lane = h * HEAD_SIZE
            rows = stack_group(query, h, half)
            key_early = early_scratch[:, lane : lane + HEAD_SIZE]
            key_late = late_scratch[:, lane : lane + HEAD_SIZE]
            value_early = early_scratch[:, KEY_WIDTH + lane : KEY_WIDTH + lane + HEAD_SIZE]
            value_late = late_scratch[:, KEY_WIDTH + lane : KEY_WIDTH + lane + HEAD_SIZE]
            score_early = jnp.where(visible_early, dot_nt(key_early, rows), -1e30)
            score_late = jnp.where(visible_late, dot_nt(key_late, rows[:wide]), -1e30)
            high_early = jnp.max(score_early, axis=0, keepdims=True)
            high_late = jnp.max(score_late, axis=0, keepdims=True)
            high_late = jnp.maximum(high_early[:, :wide], high_late)
            high = jnp.concatenate([high_late, high_early[:, wide:]], axis=1)
            raised_early = jnp.exp(score_early - high)
            raised_late = jnp.exp(score_late - high_late)
            sum_early = jnp.sum(raised_early, axis=0, keepdims=True)
            sum_late = sum_early[:, :wide] + jnp.sum(raised_late, axis=0, keepdims=True)
            total = jnp.concatenate([sum_late, sum_early[:, wide:]], axis=1)
            inverse = 1.0 / total
            mixed_early = dot_tn(value_early, (raised_early * inverse).astype(BF16))
            mixed_late = dot_tn(value_late, (raised_late * inverse[:, :wide]).astype(BF16))
            joined = jnp.concatenate(
                [mixed_early[:, :wide] + mixed_late, mixed_early[:, wide:]], axis=1
            )
            groups.append(joined.T)
            total_ref[h : h + 1, :] = high + jnp.log(total)
        mixed = unstack_groups(groups, half).astype(BF16)
        mixed_ref[...] = mixed
        for j in range(parts):
            block_scratch[own ^ j] = dot_nn(mixed, output_refs[j][...])
        middle = rows_ref[0] + jnp.concatenate(
            [block_scratch[b] for b in range(parts)], axis=1
        )
        middle_ref[...] = middle
        normed, _ = norm_of(middle)
        feed = (normed * gain_ref[...]).astype(BF16)
        block = feed.shape[-1] // parts
        for b in range(parts):
            feed_ref[b, :, :block] = feed[:, b * block : (b + 1) * block]

    return body


def row_blocks(refs, block, *index):
    return jnp.concatenate([r[index] for r in refs], axis=0)[:, :block]


def put_rows(kept_ref, sent_ref, block, values, rows):
    for i in range(values.shape[0] // rows):
        target = sent_ref if i % 2 else kept_ref
        target[i // 2, block, :, : values.shape[1]] = values[i * rows : (i + 1) * rows]


def down_weights(values):
    return [Hbm(v, (0, 2) if v.ndim == 4 else (2,)) for v in values]


def feed_weight(refs, j, m):
    return refs[2][0, m] if j == 2 else refs[j][m]


def feed_body(parts, block):
    def body(*refs):
        own = refs[0][0]
        input_refs = refs[1 : 1 + parts]
        feed_refs = refs[1 + parts : 1 + 2 * parts]
        weight_refs = refs[1 + 2 * parts : 1 + 3 * parts]
        kept_ref, sent_ref, hidden_ref, gate_ref, up_ref = refs[1 + 3 * parts :]
        rows = input_refs[0].shape[1]
        gate = up = units = None
        for j in range(parts):
            rows_in = row_blocks(input_refs, block, own ^ j)
            feed = row_blocks(feed_refs, block, own ^ j)
            terms = [
                dot_nn(rows_in, feed_weight(weight_refs, j, 0)),
                dot_nn(rows_in, feed_weight(weight_refs, j, 1)),
                dot_nn(feed, feed_weight(weight_refs, j, 2)),
            ]
            if gate is None:
                gate, up, units = terms
            else:
                gate, up, units = gate + terms[0], up + terms[1], units + terms[2]
        sigmoid = 1.0 / (1.0 + jnp.exp(-gate))
        silu = gate * sigmoid
        hidden_ref[...] = (silu * up).astype(BF16)
        grad_up = (units * silu).astype(BF16)
        grad_gate = (units * up * sigmoid * (1.0 + gate * (1.0 - sigmoid))).astype(BF16)
        gate_ref[...] = grad_gate
        up_ref[...] = grad_up
        for j in range(parts):
            back = dot_nt(grad_gate, feed_weight(weight_refs, j, 0))
            back = back + dot_nt(grad_up, feed_weight(weight_refs, j, 1))
            put_rows(kept_ref, sent_ref, own ^ j, back.astype(BF16), rows)

    return body


def put_units(kept_ref, sent_ref, first, at, values, count):
    share = values.shape[0] // count
    for c in range(0, count, 2):
        even = values[c * share : (c + 1) * share]
        odd = values[(c + 1) * share : (c + 2) * share]
        kept_ref[c // 2, at : at + share] = jnp.where(first, even, odd).astype(BF16)
        sent_ref[c // 2, at : at + share] = jnp.where(first, odd, even).astype(BF16)


def feed_grads_body(parts, count, block):
    def body(*refs):
        own = refs[0][0]
        first = refs[1][0] == 0
        input_refs = refs[2 : 2 + parts]
        feed_refs = refs[2 + parts : 2 + 2 * parts]
        left_refs = refs[2 + 2 * parts : 5 + 2 * parts]
        grad_refs = refs[5 + 2 * parts :]
        share = left_refs[0].shape[1] // count
        for m in range(3):
            kept_ref, sent_ref = grad_refs[2 * m : 2 * m + 2]
            for j in range(parts):
                rows_in = row_blocks(input_refs if m else feed_refs, block, own ^ j)
                grads = dot_tn(left_refs[m][...], rows_in)
                put_units(kept_ref, sent_ref, first, j * share, grads, count)
            sent_ref.flush()
            kept_ref.flush()

    return body


def feed_out_body(parts, rows):
    def body(*refs):
        own = refs[0][0]
        weight_refs = refs[1 : 1 + parts]
        hidden_ref, kept_out, sent_out = refs[1 + parts :]
        for j in range(parts):
            out = dot_nt(hidden_ref[...], weight_refs[j][...]).astype(BF16)
            put_rows(kept_out, sent_out, own ^ j, out, rows)

    return body


def gate_up_grads_body(parts, count, block):
    def body(*refs):
        own = refs[0][0]
        first = refs[1][0] == 0
        input_refs = refs[2 : 2 + parts]
        left_refs = refs[2 + parts : 4 + parts]
        grad_refs = refs[4 + parts :]
        for m in range(2):
            for j in range(parts):
                grads = dot_tn(left_refs[m][...], row_blocks(input_refs, block, own ^ j))
                put_units(grad_refs[2 * m], grad_refs[2 * m + 1], first, j, grads, count)
            grad_refs[2 * m + 1].flush()
            grad_refs[2 * m].flush()

    return body


def joined_blocks(kept_ref, received_ref, passed_ref, parts, block):
    return jnp.concatenate(
        [
            (
                kept_ref[0, b].astype(F32)
                + received_ref[0, b].astype(F32)
                + passed_ref[b].astype(F32)
            )[:, :block]
            for b in range(parts)
        ],
        axis=1,
    )


def back_body(parts, count, half, block):
    wide = GROUP * half

    def body(*refs):
        own = refs[0][0]
        (
            kept_ref,
            received_ref,
            passed_ref,
            middle_ref,
            gain_ref,
            rows_ref,
            mixed_ref,
            query_ref,
            total_ref,
            early_pos,
            late_pos,
            row_pos,
            cosine_ref,
            sine_ref,
        ) = refs[1:15]
        pair_refs = refs[15 : 15 + count]
        output_refs = refs[15 + count : 15 + count + parts]
        at = 15 + count + parts
        grad_middle_ref, pack_ref, gain_grad_ref = refs[at : at + 3]
        grad_pair_refs = refs[at + 3 : at + 5]
        early_scratch, late_scratch = refs[at + 5 :]
        split_keys(pair_refs, early_scratch, late_scratch, half)
        normed, factor = norm_of(middle_ref[...])
        grad = joined_blocks(kept_ref, received_ref, passed_ref, parts, block)
        gain_grad_ref[...] = jnp.sum(grad * normed, axis=0, keepdims=True)
        scaled = grad * gain_ref[...]
        grad_middle = rows_ref[1] + factor * (
            scaled - normed * jnp.mean(scaled * normed, axis=-1, keepdims=True)
        )
        grad_middle_ref[...] = grad_middle
        mixed_in = grad_middle.astype(BF16)
        for b in range(parts):
            pack_ref[1, b, :, :block] = mixed_ref[:, b * block : (b + 1) * block]
            pack_ref[2, b, :, :block] = mixed_in[:, b * block : (b + 1) * block]
        mixed_grad = None
        for j in range(parts):
            term = dot_nt(pack_ref[2, own ^ j][:, :block], output_refs[j][...])
            mixed_grad = term if mixed_grad is None else mixed_grad + term
        mixed_grad = mixed_grad.astype(BF16)
        product = mixed_grad.astype(F32) * mixed_ref[...].astype(F32)
        query = query_ref[...] * SCALE
        visible_early = early_pos[...] <= row_pos[...]
        visible_late = late_pos[...] <= row_pos[:, :wide]
        groups = []
        grads_early = [[], []]
        grads_late = [[], []]
        for h in range(KEY_HEADS):
            lane = h * HEAD_SIZE
            rows = stack_group(query, h, half)
            outer = stack_group(mixed_grad, h, half)
            delta = jnp.sum(stack_group(product, h, half).T, axis=0, keepdims=True)
            log_total = total_ref[h : h + 1, :]
            key_early = early_scratch[:, lane : lane + HEAD_SIZE]
            key_late = late_scratch[:, lane : lane + HEAD_SIZE]
            value_early = early_scratch[:, KEY_WIDTH + lane : KEY_WIDTH + lane + HEAD_SIZE]
            value_late = late_scratch[:, KEY_WIDTH + lane : KEY_WIDTH + lane + HEAD_SIZE]
            probs = jnp.where(visible_early, jnp.exp(dot_nt(key_early, rows) - log_total), 0.0)
            score_grad = (probs * (dot_nt(value_early, outer) - delta)).astype(BF16)
            grads_early[1].append(dot_nn(probs.astype(BF16), outer))
            grads_early[0].append(dot_nn(score_grad, rows))
            query_early = dot_tn(key_early, score_grad)
            probs = jnp.where(
                visible_late, jnp.exp(dot_nt(key_late, rows[:wide]) - log_total[:, :wide]), 0.0
            )
            score_grad = (probs * (dot_nt(value_late, outer[:wide]) - delta[:, :wide])).astype(BF16)
            grads_late[1].append(dot_nn(probs.astype(BF16), outer[:wide]))
            grads_late[0].append(dot_nn(score_grad, rows[:wide]))
            query_late = dot_tn(key_late, score_grad)
            joined = jnp.concatenate(
                [query_early[:, :wide] + query_late, query_early[:, wide:]], axis=1
            )
            groups.append(joined.T)
        grad_query = unstack_groups(groups, half) * SCALE
        padded = jnp.concatenate([grad_query, jnp.zeros_like(grad_query[:, :HEAD_SIZE])], axis=1)
        padded = rotated(padded, cosine_ref[...], -sine_ref[...]).astype(BF16)
        for b in range(parts):
            pack_ref[0, b, :, :block] = padded[:, b * block : (b + 1) * block]
        pair_early = jnp.concatenate(grads_early[0] + grads_early[1], axis=1).astype(BF16)
        pair_late = jnp.concatenate(grads_late[0] + grads_late[1], axis=1).astype(BF16)
        for j in range(count):
            grad_pair_refs[j % 2][j // 2, :half, :] = pair_early[j * half : (j + 1) * half]
            grad_pair_refs[j % 2][j // 2, half:, :] = pair_late[j * half : (j + 1) * half]

    return body


def attention_grads_body(parts, count, block):
    def body(*refs):
        own = refs[0][0]
        first = refs[1][0] == 0
        pack_refs = refs[2 : 2 + parts]
        input_refs = refs[2 + parts : 2 + 2 * parts]
        kept_ref, sent_ref = refs[2 + 2 * parts :]
        inputs = row_blocks(input_refs, block, own)
        mixed_in = row_blocks(pack_refs, block, 2, own)
        grads = [
            jnp.concatenate(
                [dot_tn(row_blocks(pack_refs, block, m, b), right) for b in range(parts)], axis=0
            )
            for m, right in ((0, inputs), (1, mixed_in))
        ]
        put_groups(kept_ref, sent_ref, first, 0, grads, count)

    return body


def put_groups(kept_ref, sent_ref, first, at, grads, count):
    def rows_of(c):
        pieces = []
        for values in grads:
            rows = values.shape[0] // count
            pieces.append(values[c * rows : (c + 1) * rows])
        return jnp.concatenate(pieces, axis=0)

    for c in range(0, count, 2):
        even, odd = rows_of(c), rows_of(c + 1)
        stop = at + even.shape[0]
        kept_ref[c // 2, at:stop] = jnp.where(first, even, odd).astype(BF16)
        sent_ref[c // 2, at:stop] = jnp.where(first, odd, even).astype(BF16)


def output_body(parts, block):
    def body(middle_ref, kept_ref, received_ref, passed_ref, out_ref):
        out = middle_ref[...] + joined_blocks(kept_ref, received_ref, passed_ref, parts, block)
        out_ref[...] = out.T

    return body


def input_grad_body(parts, block):
    def body(*refs):
        own = refs[0][0]
        pair_kept, pair_received, cosine_ref, sine_ref, pack_ref, rows_ref, gain_ref = refs[1:8]
        middle_ref = refs[8]
        weight_refs = refs[9 : 9 + parts]
        pair_ref, grad_ref, gain_grad_ref, block_scratch = refs[9 + parts :]
        pair = pair_kept[0].astype(F32) + pair_received[0].astype(F32)
        turned = rotated(pair, cosine_ref[...], -sine_ref[...])
        pair = jnp.concatenate([turned[:, :KEY_WIDTH], pair[:, KEY_WIDTH:]], axis=1).astype(BF16)
        pair_ref[...] = pair
        grads = [pack_ref[0, b][:, :block] for b in range(parts)] + [pair]
        grads = jnp.concatenate(grads, axis=1)
        for j in range(parts):
            block_scratch[own ^ j] = dot_nt(grads, weight_refs[j][...])
        grad = jnp.concatenate([block_scratch[b] for b in range(parts)], axis=1)
        normed, factor = norm_of(rows_ref[0])
        gain_grad_ref[...] = jnp.sum(grad * normed, axis=0, keepdims=True)
        scaled = grad * gain_ref[...]
        result = middle_ref[...] + factor * (
            scaled - normed * jnp.mean(scaled * normed, axis=-1, keepdims=True)
        )
        grad_ref[...] = result.T

    return body


def pair_grads_body(parts, count, block):
    def body(*refs):
        own = refs[0][0]
        first = refs[1][0] == 0
        pair_refs = refs[2 : 2 + parts]
        acts_refs = refs[2 + parts : 2 + 2 * parts]
        kept_ref, sent_ref = refs[2 + 2 * parts :]
        pairs = jnp.concatenate([r[...] for r in pair_refs], axis=0)
        grads = dot_tn(pairs, row_blocks(acts_refs, block, own))
        put_groups(kept_ref, sent_ref, first, 0, [grads[:KEY_WIDTH], grads[KEY_WIDTH:]], count)

    return body


def shards(
    block_input,
    pair_of_device,
    query_weight,
    key_weight,
    value_matrix,
    output_weight,
    gate_weight,
    up_weight,
    down_weight,
    attention_gain,
    feedforward_gain,
    output_cotangent,
):
    hidden = block_input[0]
    cotangent = output_cotangent[0]
    rows, width = hidden.shape
    half = rows // 2
    count = lax.axis_size("ctx")
    parts = lax.axis_size("fsdp")
    own_ctx = lax.axis_index("ctx")
    own = lax.axis_index("fsdp")
    block = width // parts
    padded = -(-block // 128) * 128
    units = down_weight.shape[1]
    share = units // (count * parts)
    own_scalar = own.astype(jnp.int32).reshape(1)

    device_ids = jnp.arange(count, dtype=jnp.int32)
    relative = own_ctx.astype(jnp.int32) ^ device_ids
    pairs = jnp.sum(
        jnp.where(relative[:, None] == device_ids[None, :], pair_of_device[None, :], 0), axis=1
    )
    within = jnp.arange(half, dtype=jnp.int32)
    early_pos = (pairs[:, None] * half + within[None, :]).reshape(-1, 1)
    late_pos = ((2 * count - 1 - pairs)[:, None] * half + within[None, :]).reshape(-1, 1)
    own_early = pairs[0] * half + within
    own_late = (2 * count - 1 - pairs[0]) * half + within
    row_pos = jnp.concatenate([own_late] * GROUP + [own_early] * GROUP)[None, :]
    half_head = HEAD_SIZE // 2
    frequency = jnp.exp(
        jnp.arange(half_head, dtype=F32) * (-2.0 * math.log(THETA) / HEAD_SIZE)
    )
    positions = jnp.concatenate([own_early, own_late])
    angles = positions.astype(F32)[:, None] * frequency[None, :]
    cosine, sine = jnp.cos(angles), jnp.sin(angles)
    cosine = jnp.concatenate([cosine] * 4, axis=1)
    sine = jnp.concatenate([-sine, sine] * 2, axis=1)

    side_scalar = (own_ctx & 1).astype(jnp.int32).reshape(1)
    hidden_count = count * share

    weight_pack, attend_input, grad_feed, both_rows = launch(
        prepare_body(parts),
        [
            ((block, QUERY_WIDTH + 2 * KEY_WIDTH), BF16, True),
            ((parts, rows, padded), BF16),
            ((parts, rows, padded), BF16),
            ((2, rows, width), F32),
        ],
        [],
        [
            hidden.T,
            cotangent.T,
            attention_gain,
            query_weight[0],
            key_weight[0].T,
            value_matrix[0].T,
        ],
    )
    weight_far = swap(weight_pack, "fsdp", 2)
    weight_near = swap(weight_pack, "fsdp", 1)

    gate_now, up_now, down_now, _ = lax.optimization_barrier(
        (gate_weight, up_weight, down_weight, weight_pack)
    )
    piece_own, piece_near, piece_far = launch(
        deal_body(parts, count),
        [
            ((3, block, hidden_count), BF16),
            ((3, block, hidden_count), BF16),
            ((2, 3, block, hidden_count), BF16),
        ],
        [own_scalar],
        hbm([gate_now[0], up_now[0], down_now[0].T]),
        [pltpu.VMEM((parts, block, hidden_count), BF16)],
    )
    tables = (cosine, sine, early_pos, late_pos, row_pos)
    output_now, weight_far, weight_near, piece_far, tables = lax.optimization_barrier(
        (output_weight[0], weight_far, weight_near, piece_far, tables)
    )
    cosine, sine, early_pos, late_pos, row_pos = tables
    weights = [weight_pack, weight_near, weight_far, swap(weight_far, "fsdp", 1)]
    output_far = swap(output_now, "fsdp", 2)
    query, key_value = launch(
        project_body(parts, block),
        [((rows, QUERY_WIDTH), BF16), ((rows, 2 * KEY_WIDTH), BF16)],
        [own_scalar],
        [attend_input, cosine, sine, *hbm(weights)],
    )
    output_far, far_now = lax.optimization_barrier((output_far, piece_far, key_value))[:2]
    feed_far = swap(far_now, "fsdp", 2)
    key_values, extras = gather_levels(
        key_value,
        "ctx",
        [
            lambda token: (
                swap(after(output_now, token), "fsdp", 1),
                swap(after(piece_near, token), "fsdp", 1),
            ),
            lambda token: (swap(after(output_far, token), "fsdp", 1),),
        ],
    )
    output_blocks = [output_now, extras[0][0], output_far, extras[1][0]]
    feed_near = extras[0][1]
    feeds_far = swap(after(grad_feed, key_values[-2]), "fsdp", 2)

    mixed, log_total, middle, feed_input = launch(
        attend_body(parts, count, half),
        [
            ((rows, QUERY_WIDTH), BF16),
            ((KEY_HEADS, 2 * GROUP * half), F32),
            ((rows, width), F32),
            ((parts, rows, padded), BF16),
        ],
        [own_scalar],
        [
            query,
            early_pos,
            late_pos,
            row_pos,
            both_rows,
            feedforward_gain,
            *key_values,
            *hbm(output_blocks),
        ],
        [
            pltpu.VMEM((count * half, 2 * KEY_WIDTH), BF16),
            pltpu.VMEM((count * half, 2 * KEY_WIDTH), BF16),
            pltpu.VMEM((parts, rows, block), F32),
        ],
    )
    input_far = swap(feed_input, "fsdp", 2)
    near_now, far_now, feed_far = lax.optimization_barrier(
        (grad_feed, feeds_far, feed_far, input_far)
    )[:3]
    feeds = [grad_feed, swap(near_now, "fsdp", 1), feeds_far, swap(far_now, "fsdp", 1)]
    feed_weights = [piece_own, feed_near, feed_far, swap(feed_far[1], "fsdp", 1)]
    feed_inputs = [
        feed_input,
        swap(feed_input, "fsdp", 1),
        input_far,
        swap(input_far, "fsdp", 1),
    ]
    kept, sent, hidden_units, grad_gate, grad_up = launch(
        feed_body(parts, block),
        [((2, parts, rows, padded), BF16)] * 2 + [((parts * rows, hidden_count), BF16)] * 3,
        [own_scalar],
        [*feed_inputs, *feeds, *hbm(feed_weights)],
    )
    received = swap(sent, "fsdp", 1)
    passed = (kept[1].astype(F32) + received[1].astype(F32)).astype(BF16)
    passed, hidden_units, grad_gate, grad_up = lax.optimization_barrier(
        (passed, hidden_units, grad_gate, grad_up)
    )
    passed = swap(passed, "fsdp", 2)
    down_kept, down_sent, gate_kept, gate_sent, up_kept, up_sent = launch(
        feed_grads_body(parts, count, block),
        [((count // 2, parts * share, block), BF16, True)] * 6,
        [own_scalar, side_scalar],
        [*feed_inputs, *feeds, hidden_units, grad_gate, grad_up],
    )
    down_received = swap(down_sent, "ctx", 1)
    passed = after(passed, down_sent)
    input_far = swap(after(attend_input, passed), "fsdp", 2)

    grad_middle, pack, feed_gain_part, pair_kept, pair_sent = launch(
        back_body(parts, count, half, block),
        [((rows, width), F32), ((3, parts, rows, padded), BF16, True), ((1, width), F32)]
        + [((count // 2, rows, 2 * KEY_WIDTH), BF16)] * 2,
        [own_scalar],
        [
            kept,
            received,
            passed,
            middle,
            feedforward_gain,
            both_rows,
            mixed,
            query,
            log_total,
            early_pos,
            late_pos,
            row_pos,
            cosine,
            sine,
            *key_values,
            *hbm(output_blocks),
        ],
        [
            pltpu.VMEM((count * half, 2 * KEY_WIDTH), BF16),
            pltpu.VMEM((count * half, 2 * KEY_WIDTH), BF16),
        ],
    )

    bits = bits_of("ctx")
    pair_sent, input_near, input_far, hidden_units, down_received = lax.optimization_barrier(
        (pair_sent, attend_input, input_far, hidden_units, down_received)
    )
    pair_received = swap(pair_sent, "ctx", 1)

    def next_step(kept, received, k, *gates):
        received = after(received, *gates)
        total = (kept.astype(F32) + received.astype(F32)).astype(BF16)
        kept, sent = split_side(total, own_ctx, k + 1)
        return kept, sent, swap(sent, "ctx", bits[k + 1])

    def last_step(kept, received, k, *gates):
        received = after(received, *gates)
        for n in range(k, len(bits) - 1):
            kept, _, received = next_step(kept, received, n)
        return (kept.astype(F32) + received.astype(F32))[0]

    pack_far = swap(pack, "fsdp", 2)
    pack_near = swap(pack, "fsdp", 1)
    inputs_swapped = swap(input_near, "fsdp", 1), swap(input_far, "fsdp", 1)
    down_kept, down_sent, down_received = next_step(down_kept, down_received, 0)
    out_kept, out_sent = launch(
        feed_out_body(parts, rows),
        [((2, parts, rows, padded), BF16)] * 2,
        [own_scalar],
        [*down_weights(feed_weights), hidden_units],
    )
    pair_received, pack_far, pack_near, inputs_swapped, out_sent, _ = lax.optimization_barrier(
        (pair_received, pack_far, pack_near, inputs_swapped, out_sent, down_sent)
    )
    gate_received = swap(after(gate_sent, pair_received), "ctx", 1)
    pair_kept, pair_sent = half_step(pair_kept, pair_received)
    pair_received = swap(pair_sent, "ctx", bits[1])
    pack_far, down_received, out_sent, _ = lax.optimization_barrier(
        (pack_far, down_received, out_sent, pair_sent)
    )
    if len(bits) > 2:
        down_kept, down_sent, down_received = next_step(down_kept, down_received, 1)
    packs = [pack, pack_near, pack_far, swap(pack_far, "fsdp", 1)]
    input_all = [attend_input, inputs_swapped[0], input_far, inputs_swapped[1]]
    up_received = swap(after(up_sent, pair_received), "ctx", 1)
    rest_kept, rest_sent = launch(
        attention_grads_body(parts, count, block),
        [((count // 2, 2 * QUERY_WIDTH // count, block), BF16, True)] * 2,
        [own_scalar, side_scalar],
        [*hbm(packs), *hbm(input_all)],
    )
    pair_received, out_now, _ = lax.optimization_barrier((pair_received, out_sent, rest_sent))
    for bit in bits[2:]:
        pair_kept, pair_sent = half_step(pair_kept, pair_received)
        pair_received = swap(pair_sent, "ctx", bit)
    rest_received = swap(after(rest_sent, pair_sent), "ctx", 1)
    pair_received = after(pair_received, down_sent)
    out_received = swap(after(out_now, pair_sent), "fsdp", 1)
    pair_in, input_grad, attention_gain_part = launch(
        input_grad_body(parts, block),
        [((rows, 2 * KEY_WIDTH), BF16), ((width, rows), F32), ((1, width), F32)],
        [own_scalar],
        [
            pair_kept,
            pair_received,
            cosine,
            sine,
            pack,
            both_rows,
            attention_gain,
            grad_middle,
            *hbm(weights),
        ],
        [pltpu.VMEM((parts, rows, block), F32)],
    )
    pair_far = swap(pair_in, "fsdp", 2)
    pair_near = swap(pair_in, "fsdp", 1)
    gains = jnp.concatenate([attention_gain_part, feed_gain_part], axis=0)
    gains = gains + swap(gains, "fsdp", 2)
    gate_kept, gate_part, gate_received = next_step(gate_kept, gate_received, 0, pair_in)
    out_received = after(out_received, pair_in)
    out_passed = (out_kept[1].astype(F32) + out_received[1].astype(F32)).astype(BF16)
    pair_far, gains, _ = lax.optimization_barrier((pair_far, gains, gate_part))
    pair_all = [pair_in, pair_near, pair_far, swap(pair_far, "fsdp", 1)]
    gains = gains + swap(gains, "fsdp", 1)
    up_kept, up_part, up_received = next_step(up_kept, up_received, 0, pair_far)
    pair_all[3], gains, _ = lax.optimization_barrier((pair_all[3], gains, up_part))
    pair_grad_kept, pair_grad_sent = launch(
        pair_grads_body(parts, count, block),
        [((count // 2, 2 * KEY_WIDTH // count, block), BF16)] * 2,
        [own_scalar, side_scalar],
        [*pair_all, *hbm(input_all)],
    )
    gains = after(gains, pair_grad_sent)
    pair_grad_received = swap(pair_grad_sent, "ctx", 1)
    gains = gains + swap(gains, "ctx", 1)
    out_passed = swap(after(out_passed, pair_grad_sent), "fsdp", 2)
    gate_part = up_part = pair_grad_sent
    for k in range(1, len(bits) - 1):
        gate_kept, gate_part, gate_received = next_step(gate_kept, gate_received, k, gate_part)
        up_kept, up_part, up_received = next_step(up_kept, up_received, k, gate_part)
    down_own = last_step(down_kept, down_received, min(2, len(bits) - 1), pair_grad_sent)
    for k in range(len(bits) - 1):
        rest_kept, rest_part, rest_received = next_step(
            rest_kept, rest_received, k, pair_grad_sent
        )
        pair_grad_kept, pair_grad_sent, pair_grad_received = next_step(
            pair_grad_kept, pair_grad_received, k, rest_part
        )
        gains = after(gains, pair_grad_sent)
        gains = gains + swap(gains, "ctx", bits[k + 1])
    middle = after(middle, up_part)
    gate_own = (gate_kept.astype(F32) + gate_received.astype(F32))[0]
    up_own = (up_kept.astype(F32) + up_received.astype(F32))[0]
    rest_own = (rest_kept.astype(F32) + rest_received.astype(F32))[0]
    pair_own = (pair_grad_kept.astype(F32) + pair_grad_received.astype(F32))[0]
    (block_output,) = launch(
        output_body(parts, block),
        [((width, rows), F32)],
        [],
        [middle, out_kept, out_received, out_passed],
    )
    query_rows, key_rows = QUERY_WIDTH // count, KEY_WIDTH // count
    query_own, output_own = rest_own[:query_rows], rest_own[query_rows:]

    stacked = jnp.concatenate([down_own, gate_own, up_own], axis=0).astype(BF16)
    stacked = stacked.reshape(3, parts, share, block).transpose(1, 0, 2, 3)
    arrived = jnp.stack(exchange_blocks([stacked[j] for j in range(parts)], "fsdp"))
    ordered = jnp.concatenate(
        [lax.dynamic_index_in_dim(arrived, own ^ b, 0, keepdims=False) for b in range(parts)],
        axis=1,
    ).astype(F32)

    return (
        block_output.T[None],
        input_grad.T[None],
        query_own.T[None],
        pair_own[:key_rows].T[None],
        pair_own[key_rows:].T[None],
        output_own[None],
        ordered[1].T[None],
        ordered[2].T[None],
        ordered[0][None],
        gains[:1],
        gains[1:],
    )


def solution(mesh):
    return jax.shard_map(
        shards,
        mesh=mesh,
        in_specs=(
            P("fsdp", "ctx", None),
            P(),
            P(None, "fsdp", None),
            P(None, "fsdp", None),
            P(None, "fsdp", None),
            P(None, None, "fsdp"),
            P(None, "fsdp", None),
            P(None, "fsdp", None),
            P(None, None, "fsdp"),
            P(),
            P(),
            P("fsdp", "ctx", None),
        ),
        out_specs=(
            P("fsdp", "ctx", None),
            P("fsdp", "ctx", None),
            P(None, "fsdp", "ctx"),
            P(None, "fsdp", "ctx"),
            P(None, "fsdp", "ctx"),
            P(None, "ctx", "fsdp"),
            P(None, "fsdp", "ctx"),
            P(None, "fsdp", "ctx"),
            P(None, "ctx", "fsdp"),
            P(),
            P(),
        ),
        check_vma=False,
    )
```

```python
import math

import jax
import jax.numpy as jnp
from jax import lax
from jax.experimental import pallas as pl
from jax.experimental.pallas import tpu as pltpu
from jax.sharding import PartitionSpec as P

QUERY_HEADS = 15
KEY_HEADS = 5
HEAD_SIZE = 64
GROUP = QUERY_HEADS // KEY_HEADS
QUERY_WIDTH = QUERY_HEADS * HEAD_SIZE
KEY_WIDTH = KEY_HEADS * HEAD_SIZE
EPSILON = 1e-05
THETA = 100000.0
SCALE = 1.0 / math.sqrt(HEAD_SIZE)
F32 = jnp.float32
BF16 = jnp.bfloat16


def dot_nn(left, right):
    return lax.dot_general(left, right, (((1,), (0,)), ((), ())), preferred_element_type=F32)


def dot_nt(left, right):
    return lax.dot_general(left, right, (((1,), (1,)), ((), ())), preferred_element_type=F32)


def dot_tn(left, right):
    return lax.dot_general(left, right, (((0,), (0,)), ((), ())), preferred_element_type=F32)


def swap(value, axis, bit):
    size = lax.axis_size(axis)
    return lax.ppermute(value, axis, [(i, i ^ bit) for i in range(size)])


def bits_of(axis):
    size = lax.axis_size(axis)
    result = []
    bit = 1
    while bit < size:
        result.append(bit)
        bit *= 2
    return result


def gather_blocks(value, axis):
    blocks = {0: value}
    order = [0]
    for bit in reversed(bits_of(axis)):
        for j in list(order):
            blocks[j ^ bit] = swap(blocks[j], axis, bit)
            order.append(j ^ bit)
    return [blocks[j] for j in range(len(order))]


def gather_levels(value, axis, beside):
    count = lax.axis_size(axis)
    blocks = {0: value}
    level = [0]
    extras = []
    while len(blocks) < count:
        width = bin(level[0]).count("1") + 1
        token = blocks[level[-1]]
        level = [j for j in range(count) if bin(j).count("1") == width]
        for j in sorted(level, reverse=True):
            blocks[j] = swap(blocks[j & (j - 1)], axis, j & -j)
        extra = beside[width - 1](token) if width <= len(beside) else ()
        gated, extra = lax.optimization_barrier((tuple(blocks[j] for j in level), extra))
        blocks.update(zip(level, gated))
        extras.append(extra)
    return [blocks[j] for j in range(count)], extras


def exchange_blocks(blocks, axis):
    return [blocks[0]] + [swap(blocks[j], axis, j) for j in range(1, len(blocks))]


def split_side(value, own, k):
    pairs = value.reshape(value.shape[0] // 2, 2, *value.shape[1:])
    side = (own >> k) & 1
    kept = lax.dynamic_index_in_dim(pairs, side, 1, keepdims=False)
    return kept, lax.dynamic_index_in_dim(pairs, 1 - side, 1, keepdims=False)


def half_step(kept, received):
    total = (kept.astype(F32) + received.astype(F32)).astype(BF16)
    pairs = total.reshape(total.shape[0] // 2, 2, *total.shape[1:])
    return pairs[:, 0], pairs[:, 1]


class Hbm:
    def __init__(self, value, index=()):
        self.value, self.index = value, index


def hbm(values):
    return [Hbm(v) for v in values]


class LateInput:
    def __init__(self, buffer, copy):
        self.buffer, self.copy, self.waiting = buffer, copy, True

    def ready(self):
        if self.waiting:
            self.copy.wait()
            self.waiting = False

    @property
    def shape(self):
        return self.buffer.shape

    def __getitem__(self, index):
        self.ready()
        return self.buffer[index]


class LateOutput:
    def __init__(self, buffer, copy):
        self.buffer, self.copy, self.started = buffer, copy, False

    def flush(self):
        if not self.started:
            self.copy.start()
            self.started = True

    def __getitem__(self, index):
        return self.buffer[index]

    def __setitem__(self, index, value):
        self.buffer[index] = value


def launch(body, outs, scalars, arrays, scratch=()):
    late_in = [isinstance(a, Hbm) for a in arrays]
    values = [a.value if isinstance(a, Hbm) else a for a in arrays]
    picks = [a.index if isinstance(a, Hbm) else () for a in arrays]
    late_out = [len(o) == 3 for o in outs]
    count_in, count_out = sum(late_in), sum(late_out)
    vmem = pl.BlockSpec(memory_space=pltpu.VMEM)
    away = pl.BlockSpec(memory_space=pl.ANY)
    buffers = [
        pltpu.VMEM(v.shape[len(p) :], v.dtype) for v, p, late in zip(values, picks, late_in) if late
    ]
    buffers += [pltpu.VMEM(o[0], o[1]) for o, late in zip(outs, late_out) if late]
    if buffers:
        buffers.append(pltpu.SemaphoreType.DMA((count_in + count_out,)))

    def wrapped(*refs):
        at = len(scalars)
        items = list(refs[:at])
        ins = refs[at : at + len(values)]
        at += len(values)
        results = refs[at : at + len(outs)]
        at += len(outs)
        own_scratch = refs[at : at + len(scratch)]
        spare = list(refs[at + len(scratch) :])
        late_ins, late_outs = [], []
        slot = 0
        for ref, pick, late in zip(ins, picks, late_in):
            if late:
                source = ref.at[pick] if pick else ref
                copy = pltpu.make_async_copy(source, spare[slot], spare[-1].at[slot])
                copy.start()
                late_ins.append(LateInput(spare[slot], copy))
                items.append(late_ins[-1])
                slot += 1
            else:
                items.append(ref)
        for ref, late in zip(results, late_out):
            if late:
                copy = pltpu.make_async_copy(spare[slot], ref, spare[-1].at[slot])
                late_outs.append(LateOutput(spare[slot], copy))
                items.append(late_outs[-1])
                slot += 1
            else:
                items.append(ref)
        body(*items, *own_scratch)
        for item in late_ins:
            item.ready()
        for item in late_outs:
            item.flush()
        for item in late_outs:
            item.copy.wait()

    return pl.pallas_call(
        wrapped,
        out_shape=[jax.ShapeDtypeStruct(o[0], o[1]) for o in outs],
        in_specs=[pl.BlockSpec(memory_space=pltpu.SMEM) for _ in scalars]
        + [away if late else vmem for late in late_in],
        out_specs=[away if late else vmem for late in late_out],
        scratch_shapes=list(scratch) + buffers,
        compiler_params=pltpu.CompilerParams(vmem_limit_bytes=60 * 1024 * 1024),
    )(*scalars, *values)


def after(value, *others):
    return lax.optimization_barrier((value, *others))[0]


def rotated(values, cosine, sine):
    width = values.shape[-1]
    lane = lax.broadcasted_iota(jnp.int32, values.shape, 1)
    ahead = pltpu.roll(values, width - HEAD_SIZE // 2, 1)
    behind = pltpu.roll(values, HEAD_SIZE // 2, 1)
    other = jnp.where((lane % HEAD_SIZE) < HEAD_SIZE // 2, ahead, behind)
    repeat = width // cosine.shape[-1]
    return values * jnp.tile(cosine, (1, repeat)) + other * jnp.tile(sine, (1, repeat))


def norm_of(hidden):
    factor = lax.rsqrt(jnp.mean(hidden * hidden, axis=-1, keepdims=True) + EPSILON)
    return hidden * factor, factor


def prepare_body(parts):
    def body(*refs):
        hidden_ref, cotangent_ref, gain_ref, query_ref, key_ref, value_ref = refs[:6]
        weight_ref, input_ref, feed_ref, rows_ref = refs[6:]
        weight_ref[...] = jnp.concatenate(
            [query_ref[...], key_ref[...].T, value_ref[...].T], axis=1
        )
        weight_ref.flush()
        hidden = hidden_ref[...].T
        cotangent = cotangent_ref[...].T
        rows_ref[0] = hidden
        rows_ref[1] = cotangent
        normed, _ = norm_of(hidden)
        attend = (normed * gain_ref[...]).astype(BF16)
        feed = cotangent.astype(BF16)
        block = attend.shape[-1] // parts
        for b in range(parts):
            input_ref[b, :, :block] = attend[:, b * block : (b + 1) * block]
            feed_ref[b, :, :block] = feed[:, b * block : (b + 1) * block]

    return body


def deal_body(parts, count):
    def body(*refs):
        own = refs[0][0]
        weight_refs = refs[1:4]
        own_ref, near_ref, far_ref, scratch = refs[4:]
        for m in range(3):
            values = weight_refs[m][...]
            chunk = values.shape[1] // count
            share = chunk // parts
            for g in range(parts):
                scratch[g] = jnp.concatenate(
                    [
                        values[:, c * chunk + g * share : c * chunk + (g + 1) * share]
                        for c in range(count)
                    ],
                    axis=1,
                )
            far_ref[0, m] = scratch[own ^ 2]
            far_ref[1, m] = scratch[own ^ 3]
            own_ref[m] = scratch[own]
            near_ref[m] = scratch[own ^ 1]

    return body


def project_body(parts, block):
    def body(*refs):
        own = refs[0][0]
        input_ref, cosine_ref, sine_ref = refs[1:4]
        weight_refs = refs[4 : 4 + parts]
        query_ref, pair_ref = refs[4 + parts :]
        result = None
        for j in range(parts):
            term = dot_nn(input_ref[own ^ j][:, :block], weight_refs[j][...])
            result = term if result is None else result + term
        both = rotated(result[:, : QUERY_WIDTH + KEY_WIDTH], cosine_ref[...], sine_ref[...])
        both = both.astype(BF16)
        query_ref[...] = both[:, :QUERY_WIDTH]
        pair_ref[:, :KEY_WIDTH] = both[:, QUERY_WIDTH:]
        pair_ref[:, KEY_WIDTH:] = result[:, QUERY_WIDTH + KEY_WIDTH :].astype(BF16)

    return body


def stack_group(values, head, half):
    pieces = []
    for start in (half, 0):
        for g in range(GROUP):
            lane = (head * GROUP + g) * HEAD_SIZE
            pieces.append(values[start : start + half, lane : lane + HEAD_SIZE])
    return jnp.concatenate(pieces, axis=0)


def unstack_groups(groups, half):
    late = [g[i * half : (i + 1) * half] for g in groups for i in range(GROUP)]
    early = [g[(GROUP + i) * half : (GROUP + i + 1) * half] for g in groups for i in range(GROUP)]
    return jnp.concatenate(
        [jnp.concatenate(early, axis=1), jnp.concatenate(late, axis=1)], axis=0
    )


def split_keys(pair_refs, early_scratch, late_scratch, half):
    for j, pair_ref in enumerate(pair_refs):
        early_scratch[j * half : (j + 1) * half, :] = pair_ref[:half, :]
        late_scratch[j * half : (j + 1) * half, :] = pair_ref[half:, :]


def attend_body(parts, count, half):
    wide = GROUP * half

    def body(*refs):
        own = refs[0][0]
        query_ref, early_pos, late_pos, row_pos, rows_ref, gain_ref = refs[1:7]
        pair_refs = refs[7 : 7 + count]
        output_refs = refs[7 + count : 7 + count + parts]
        mixed_ref, total_ref, middle_ref, feed_ref = refs[7 + count + parts : 11 + count + parts]
        early_scratch, late_scratch, block_scratch = refs[11 + count + parts :]
        split_keys(pair_refs, early_scratch, late_scratch, half)
        query = query_ref[...] * SCALE
        visible_early = early_pos[...] <= row_pos[...]
        visible_late = late_pos[...] <= row_pos[:, :wide]
        groups = []
        for h in range(KEY_HEADS):
            lane = h * HEAD_SIZE
            rows = stack_group(query, h, half)
            key_early = early_scratch[:, lane : lane + HEAD_SIZE]
            key_late = late_scratch[:, lane : lane + HEAD_SIZE]
            value_early = early_scratch[:, KEY_WIDTH + lane : KEY_WIDTH + lane + HEAD_SIZE]
            value_late = late_scratch[:, KEY_WIDTH + lane : KEY_WIDTH + lane + HEAD_SIZE]
            score_early = jnp.where(visible_early, dot_nt(key_early, rows), -1e30)
            score_late = jnp.where(visible_late, dot_nt(key_late, rows[:wide]), -1e30)
            high_early = jnp.max(score_early, axis=0, keepdims=True)
            high_late = jnp.max(score_late, axis=0, keepdims=True)
            high_late = jnp.maximum(high_early[:, :wide], high_late)
            high = jnp.concatenate([high_late, high_early[:, wide:]], axis=1)
            raised_early = jnp.exp(score_early - high)
            raised_late = jnp.exp(score_late - high_late)
            sum_early = jnp.sum(raised_early, axis=0, keepdims=True)
            sum_late = sum_early[:, :wide] + jnp.sum(raised_late, axis=0, keepdims=True)
            total = jnp.concatenate([sum_late, sum_early[:, wide:]], axis=1)
            inverse = 1.0 / total
            mixed_early = dot_tn(value_early, (raised_early * inverse).astype(BF16))
            mixed_late = dot_tn(value_late, (raised_late * inverse[:, :wide]).astype(BF16))
            joined = jnp.concatenate(
                [mixed_early[:, :wide] + mixed_late, mixed_early[:, wide:]], axis=1
            )
            groups.append(joined.T)
            total_ref[h : h + 1, :] = high + jnp.log(total)
        mixed = unstack_groups(groups, half).astype(BF16)
        mixed_ref[...] = mixed
        for j in range(parts):
            block_scratch[own ^ j] = dot_nn(mixed, output_refs[j][...])
        middle = rows_ref[0] + jnp.concatenate(
            [block_scratch[b] for b in range(parts)], axis=1
        )
        middle_ref[...] = middle
        normed, _ = norm_of(middle)
        feed = (normed * gain_ref[...]).astype(BF16)
        block = feed.shape[-1] // parts
        for b in range(parts):
            feed_ref[b, :, :block] = feed[:, b * block : (b + 1) * block]

    return body


def row_blocks(refs, block, *index):
    return jnp.concatenate([r[index] for r in refs], axis=0)[:, :block]


def put_rows(kept_ref, sent_ref, block, values, rows):
    for i in range(values.shape[0] // rows):
        target = sent_ref if i % 2 else kept_ref
        target[i // 2, block, :, : values.shape[1]] = values[i * rows : (i + 1) * rows]


def down_weights(values):
    return [Hbm(v, (0, 2) if v.ndim == 4 else (2,)) for v in values]


def feed_weight(refs, j, m):
    return refs[2][0, m] if j == 2 else refs[j][m]


def feed_body(parts, block):
    def body(*refs):
        own = refs[0][0]
        input_refs = refs[1 : 1 + parts]
        feed_refs = refs[1 + parts : 1 + 2 * parts]
        weight_refs = refs[1 + 2 * parts : 1 + 3 * parts]
        kept_ref, sent_ref, hidden_ref, gate_ref, up_ref = refs[1 + 3 * parts :]
        rows = input_refs[0].shape[1]
        gate = up = units = None
        for j in range(parts):
            rows_in = row_blocks(input_refs, block, own ^ j)
            feed = row_blocks(feed_refs, block, own ^ j)
            terms = [
                dot_nn(rows_in, feed_weight(weight_refs, j, 0)),
                dot_nn(rows_in, feed_weight(weight_refs, j, 1)),
                dot_nn(feed, feed_weight(weight_refs, j, 2)),
            ]
            if gate is None:
                gate, up, units = terms
            else:
                gate, up, units = gate + terms[0], up + terms[1], units + terms[2]
        sigmoid = 1.0 / (1.0 + jnp.exp(-gate))
        silu = gate * sigmoid
        hidden_ref[...] = (silu * up).astype(BF16)
        grad_up = (units * silu).astype(BF16)
        grad_gate = (units * up * sigmoid * (1.0 + gate * (1.0 - sigmoid))).astype(BF16)
        gate_ref[...] = grad_gate
        up_ref[...] = grad_up
        for j in range(parts):
            back = dot_nt(grad_gate, feed_weight(weight_refs, j, 0))
            back = back + dot_nt(grad_up, feed_weight(weight_refs, j, 1))
            put_rows(kept_ref, sent_ref, own ^ j, back.astype(BF16), rows)

    return body


def put_units(kept_ref, sent_ref, first, at, values, count):
    share = values.shape[0] // count
    for c in range(0, count, 2):
        even = values[c * share : (c + 1) * share]
        odd = values[(c + 1) * share : (c + 2) * share]
        kept_ref[c // 2, at : at + share] = jnp.where(first, even, odd).astype(BF16)
        sent_ref[c // 2, at : at + share] = jnp.where(first, odd, even).astype(BF16)


def feed_grads_body(parts, count, block, left_count):
    def body(*refs):
        own = refs[0][0]
        first = refs[1][0] == 0
        right_refs = refs[2 : 2 + parts]
        left_refs = refs[2 + parts : 2 + parts + left_count]
        grad_refs = refs[2 + parts + left_count :]
        share = left_refs[0].shape[1] // count
        for m in range(left_count):
            kept_ref, sent_ref = grad_refs[2 * m : 2 * m + 2]
            for j in range(parts):
                rows_in = row_blocks(right_refs, block, own ^ j)
                grads = dot_tn(left_refs[m][...], rows_in)
                put_units(kept_ref, sent_ref, first, j * share, grads, count)
            sent_ref.flush()
            kept_ref.flush()

    return body


def feed_out_body(parts, rows):
    def body(*refs):
        own = refs[0][0]
        weight_refs = refs[1 : 1 + parts]
        hidden_ref, kept_out, sent_out = refs[1 + parts :]
        for j in range(parts):
            out = dot_nt(hidden_ref[...], weight_refs[j][...]).astype(BF16)
            put_rows(kept_out, sent_out, own ^ j, out, rows)

    return body


def gate_up_grads_body(parts, count, block):
    def body(*refs):
        own = refs[0][0]
        first = refs[1][0] == 0
        input_refs = refs[2 : 2 + parts]
        left_refs = refs[2 + parts : 4 + parts]
        grad_refs = refs[4 + parts :]
        for m in range(2):
            for j in range(parts):
                grads = dot_tn(left_refs[m][...], row_blocks(input_refs, block, own ^ j))
                put_units(grad_refs[2 * m], grad_refs[2 * m + 1], first, j, grads, count)
            grad_refs[2 * m + 1].flush()
            grad_refs[2 * m].flush()

    return body


def joined_blocks(kept_ref, received_ref, passed_ref, parts, block):
    return jnp.concatenate(
        [
            (
                kept_ref[0, b].astype(F32)
                + received_ref[0, b].astype(F32)
                + passed_ref[b].astype(F32)
            )[:, :block]
            for b in range(parts)
        ],
        axis=1,
    )


def back_body(parts, count, half, block):
    wide = GROUP * half

    def body(*refs):
        own = refs[0][0]
        (
            kept_ref,
            received_ref,
            passed_ref,
            middle_ref,
            gain_ref,
            rows_ref,
            mixed_ref,
            query_ref,
            total_ref,
            early_pos,
            late_pos,
            row_pos,
            cosine_ref,
            sine_ref,
        ) = refs[1:15]
        pair_refs = refs[15 : 15 + count]
        output_refs = refs[15 + count : 15 + count + parts]
        at = 15 + count + parts
        grad_middle_ref, pack_ref, gain_grad_ref = refs[at : at + 3]
        grad_pair_refs = refs[at + 3 : at + 5]
        early_scratch, late_scratch = refs[at + 5 :]
        split_keys(pair_refs, early_scratch, late_scratch, half)
        normed, factor = norm_of(middle_ref[...])
        grad = joined_blocks(kept_ref, received_ref, passed_ref, parts, block)
        gain_grad_ref[...] = jnp.sum(grad * normed, axis=0, keepdims=True)
        scaled = grad * gain_ref[...]
        grad_middle = rows_ref[1] + factor * (
            scaled - normed * jnp.mean(scaled * normed, axis=-1, keepdims=True)
        )
        grad_middle_ref[...] = grad_middle
        mixed_in = grad_middle.astype(BF16)
        for b in range(parts):
            pack_ref[1, b, :, :block] = mixed_ref[:, b * block : (b + 1) * block]
            pack_ref[2, b, :, :block] = mixed_in[:, b * block : (b + 1) * block]
        mixed_grad = None
        for j in range(parts):
            term = dot_nt(pack_ref[2, own ^ j][:, :block], output_refs[j][...])
            mixed_grad = term if mixed_grad is None else mixed_grad + term
        mixed_grad = mixed_grad.astype(BF16)
        product = mixed_grad.astype(F32) * mixed_ref[...].astype(F32)
        query = query_ref[...] * SCALE
        visible_early = early_pos[...] <= row_pos[...]
        visible_late = late_pos[...] <= row_pos[:, :wide]
        groups = []
        grads_early = [[], []]
        grads_late = [[], []]
        for h in range(KEY_HEADS):
            lane = h * HEAD_SIZE
            rows = stack_group(query, h, half)
            outer = stack_group(mixed_grad, h, half)
            delta = jnp.sum(stack_group(product, h, half).T, axis=0, keepdims=True)
            log_total = total_ref[h : h + 1, :]
            key_early = early_scratch[:, lane : lane + HEAD_SIZE]
            key_late = late_scratch[:, lane : lane + HEAD_SIZE]
            value_early = early_scratch[:, KEY_WIDTH + lane : KEY_WIDTH + lane + HEAD_SIZE]
            value_late = late_scratch[:, KEY_WIDTH + lane : KEY_WIDTH + lane + HEAD_SIZE]
            probs = jnp.where(visible_early, jnp.exp(dot_nt(key_early, rows) - log_total), 0.0)
            score_grad = (probs * (dot_nt(value_early, outer) - delta)).astype(BF16)
            grads_early[1].append(dot_nn(probs.astype(BF16), outer))
            grads_early[0].append(dot_nn(score_grad, rows))
            query_early = dot_tn(key_early, score_grad)
            probs = jnp.where(
                visible_late, jnp.exp(dot_nt(key_late, rows[:wide]) - log_total[:, :wide]), 0.0
            )
            score_grad = (probs * (dot_nt(value_late, outer[:wide]) - delta[:, :wide])).astype(BF16)
            grads_late[1].append(dot_nn(probs.astype(BF16), outer[:wide]))
            grads_late[0].append(dot_nn(score_grad, rows[:wide]))
            query_late = dot_tn(key_late, score_grad)
            joined = jnp.concatenate(
                [query_early[:, :wide] + query_late, query_early[:, wide:]], axis=1
            )
            groups.append(joined.T)
        grad_query = unstack_groups(groups, half) * SCALE
        padded = jnp.concatenate([grad_query, jnp.zeros_like(grad_query[:, :HEAD_SIZE])], axis=1)
        padded = rotated(padded, cosine_ref[...], -sine_ref[...]).astype(BF16)
        for b in range(parts):
            pack_ref[0, b, :, :block] = padded[:, b * block : (b + 1) * block]
        pair_early = jnp.concatenate(grads_early[0] + grads_early[1], axis=1).astype(BF16)
        pair_late = jnp.concatenate(grads_late[0] + grads_late[1], axis=1).astype(BF16)
        for j in range(count):
            grad_pair_refs[j % 2][j // 2, :half, :] = pair_early[j * half : (j + 1) * half]
            grad_pair_refs[j % 2][j // 2, half:, :] = pair_late[j * half : (j + 1) * half]

    return body


def attention_grads_body(parts, count, block):
    def body(*refs):
        own = refs[0][0]
        first = refs[1][0] == 0
        pack_refs = refs[2 : 2 + parts]
        input_refs = refs[2 + parts : 2 + 2 * parts]
        kept_ref, sent_ref = refs[2 + 2 * parts :]
        inputs = row_blocks(input_refs, block, own)
        mixed_in = row_blocks(pack_refs, block, 2, own)
        grads = [
            jnp.concatenate(
                [dot_tn(row_blocks(pack_refs, block, m, b), right) for b in range(parts)], axis=0
            )
            for m, right in ((0, inputs), (1, mixed_in))
        ]
        put_groups(kept_ref, sent_ref, first, 0, grads, count)

    return body


def put_groups(kept_ref, sent_ref, first, at, grads, count):
    def rows_of(c):
        pieces = []
        for values in grads:
            rows = values.shape[0] // count
            pieces.append(values[c * rows : (c + 1) * rows])
        return jnp.concatenate(pieces, axis=0)

    for c in range(0, count, 2):
        even, odd = rows_of(c), rows_of(c + 1)
        stop = at + even.shape[0]
        kept_ref[c // 2, at:stop] = jnp.where(first, even, odd).astype(BF16)
        sent_ref[c // 2, at:stop] = jnp.where(first, odd, even).astype(BF16)


def output_body(parts, block):
    def body(middle_ref, kept_ref, received_ref, passed_ref, out_ref):
        out = middle_ref[...] + joined_blocks(kept_ref, received_ref, passed_ref, parts, block)
        out_ref[...] = out.T

    return body


def input_grad_body(parts, block):
    def body(*refs):
        own = refs[0][0]
        pair_kept, pair_received, cosine_ref, sine_ref, pack_ref, rows_ref, gain_ref = refs[1:8]
        middle_ref = refs[8]
        weight_refs = refs[9 : 9 + parts]
        pair_ref, grad_ref, gain_grad_ref, block_scratch = refs[9 + parts :]
        pair = pair_kept[0].astype(F32) + pair_received[0].astype(F32)
        turned = rotated(pair, cosine_ref[...], -sine_ref[...])
        pair = jnp.concatenate([turned[:, :KEY_WIDTH], pair[:, KEY_WIDTH:]], axis=1).astype(BF16)
        pair_ref[...] = pair
        grads = [pack_ref[0, b][:, :block] for b in range(parts)] + [pair]
        grads = jnp.concatenate(grads, axis=1)
        for j in range(parts):
            block_scratch[own ^ j] = dot_nt(grads, weight_refs[j][...])
        grad = jnp.concatenate([block_scratch[b] for b in range(parts)], axis=1)
        normed, factor = norm_of(rows_ref[0])
        gain_grad_ref[...] = jnp.sum(grad * normed, axis=0, keepdims=True)
        scaled = grad * gain_ref[...]
        result = middle_ref[...] + factor * (
            scaled - normed * jnp.mean(scaled * normed, axis=-1, keepdims=True)
        )
        grad_ref[...] = result.T

    return body


def pair_grads_body(parts, count, block):
    def body(*refs):
        own = refs[0][0]
        first = refs[1][0] == 0
        pair_refs = refs[2 : 2 + parts]
        acts_refs = refs[2 + parts : 2 + 2 * parts]
        kept_ref, sent_ref = refs[2 + 2 * parts :]
        pairs = jnp.concatenate([r[...] for r in pair_refs], axis=0)
        grads = dot_tn(pairs, row_blocks(acts_refs, block, own))
        put_groups(kept_ref, sent_ref, first, 0, [grads[:KEY_WIDTH], grads[KEY_WIDTH:]], count)

    return body


def shards(
    block_input,
    pair_of_device,
    query_weight,
    key_weight,
    value_matrix,
    output_weight,
    gate_weight,
    up_weight,
    down_weight,
    attention_gain,
    feedforward_gain,
    output_cotangent,
):
    hidden = block_input[0]
    cotangent = output_cotangent[0]
    rows, width = hidden.shape
    half = rows // 2
    count = lax.axis_size("ctx")
    parts = lax.axis_size("fsdp")
    own_ctx = lax.axis_index("ctx")
    own = lax.axis_index("fsdp")
    block = width // parts
    padded = -(-block // 128) * 128
    units = down_weight.shape[1]
    share = units // (count * parts)
    own_scalar = own.astype(jnp.int32).reshape(1)

    device_ids = jnp.arange(count, dtype=jnp.int32)
    relative = own_ctx.astype(jnp.int32) ^ device_ids
    pairs = jnp.sum(
        jnp.where(relative[:, None] == device_ids[None, :], pair_of_device[None, :], 0), axis=1
    )
    within = jnp.arange(half, dtype=jnp.int32)
    early_pos = (pairs[:, None] * half + within[None, :]).reshape(-1, 1)
    late_pos = ((2 * count - 1 - pairs)[:, None] * half + within[None, :]).reshape(-1, 1)
    own_early = pairs[0] * half + within
    own_late = (2 * count - 1 - pairs[0]) * half + within
    row_pos = jnp.concatenate([own_late] * GROUP + [own_early] * GROUP)[None, :]
    half_head = HEAD_SIZE // 2
    frequency = jnp.exp(
        jnp.arange(half_head, dtype=F32) * (-2.0 * math.log(THETA) / HEAD_SIZE)
    )
    positions = jnp.concatenate([own_early, own_late])
    angles = positions.astype(F32)[:, None] * frequency[None, :]
    cosine, sine = jnp.cos(angles), jnp.sin(angles)
    cosine = jnp.concatenate([cosine] * 4, axis=1)
    sine = jnp.concatenate([-sine, sine] * 2, axis=1)

    side_scalar = (own_ctx & 1).astype(jnp.int32).reshape(1)
    hidden_count = count * share

    weight_pack, attend_input, grad_feed, both_rows = launch(
        prepare_body(parts),
        [
            ((block, QUERY_WIDTH + 2 * KEY_WIDTH), BF16, True),
            ((parts, rows, padded), BF16),
            ((parts, rows, padded), BF16),
            ((2, rows, width), F32),
        ],
        [],
        [
            hidden.T,
            cotangent.T,
            attention_gain,
            query_weight[0],
            key_weight[0].T,
            value_matrix[0].T,
        ],
    )
    weight_far = swap(weight_pack, "fsdp", 2)
    weight_near = swap(weight_pack, "fsdp", 1)

    gate_now, up_now, down_now, _ = lax.optimization_barrier(
        (gate_weight, up_weight, down_weight, weight_pack)
    )
    piece_own, piece_near, piece_far = launch(
        deal_body(parts, count),
        [
            ((3, block, hidden_count), BF16),
            ((3, block, hidden_count), BF16),
            ((2, 3, block, hidden_count), BF16),
        ],
        [own_scalar],
        hbm([gate_now[0], up_now[0], down_now[0].T]),
        [pltpu.VMEM((parts, block, hidden_count), BF16)],
    )
    tables = (cosine, sine, early_pos, late_pos, row_pos)
    output_now, weight_far, weight_near, piece_far, tables = lax.optimization_barrier(
        (output_weight[0], weight_far, weight_near, piece_far, tables)
    )
    cosine, sine, early_pos, late_pos, row_pos = tables
    weights = [weight_pack, weight_near, weight_far, swap(weight_far, "fsdp", 1)]
    output_far = swap(output_now, "fsdp", 2)
    query, key_value = launch(
        project_body(parts, block),
        [((rows, QUERY_WIDTH), BF16), ((rows, 2 * KEY_WIDTH), BF16)],
        [own_scalar],
        [attend_input, cosine, sine, *hbm(weights)],
    )
    output_far, far_now = lax.optimization_barrier((output_far, piece_far, key_value))[:2]
    feed_far = swap(far_now, "fsdp", 2)
    key_values, extras = gather_levels(
        key_value,
        "ctx",
        [
            lambda token: (
                swap(after(output_now, token), "fsdp", 1),
                swap(after(piece_near, token), "fsdp", 1),
            ),
            lambda token: (swap(after(output_far, token), "fsdp", 1),),
        ],
    )
    output_blocks = [output_now, extras[0][0], output_far, extras[1][0]]
    feed_near = extras[0][1]
    feeds_far = swap(after(grad_feed, key_values[-2]), "fsdp", 2)

    mixed, log_total, middle, feed_input = launch(
        attend_body(parts, count, half),
        [
            ((rows, QUERY_WIDTH), BF16),
            ((KEY_HEADS, 2 * GROUP * half), F32),
            ((rows, width), F32),
            ((parts, rows, padded), BF16),
        ],
        [own_scalar],
        [
            query,
            early_pos,
            late_pos,
            row_pos,
            both_rows,
            feedforward_gain,
            *key_values,
            *hbm(output_blocks),
        ],
        [
            pltpu.VMEM((count * half, 2 * KEY_WIDTH), BF16),
            pltpu.VMEM((count * half, 2 * KEY_WIDTH), BF16),
            pltpu.VMEM((parts, rows, block), F32),
        ],
    )
    input_far = swap(feed_input, "fsdp", 2)
    near_now, far_now, feed_far = lax.optimization_barrier(
        (grad_feed, feeds_far, feed_far, input_far)
    )[:3]
    feeds = [grad_feed, swap(near_now, "fsdp", 1), feeds_far, swap(far_now, "fsdp", 1)]
    feed_weights = [piece_own, feed_near, feed_far, swap(feed_far[1], "fsdp", 1)]
    feed_inputs = [
        feed_input,
        swap(feed_input, "fsdp", 1),
        input_far,
        swap(input_far, "fsdp", 1),
    ]
    kept, sent, hidden_units, grad_gate, grad_up = launch(
        feed_body(parts, block),
        [((2, parts, rows, padded), BF16)] * 2 + [((parts * rows, hidden_count), BF16)] * 3,
        [own_scalar],
        [*feed_inputs, *feeds, *hbm(feed_weights)],
    )
    received = swap(sent, "fsdp", 1)
    passed = (kept[1].astype(F32) + received[1].astype(F32)).astype(BF16)
    passed, hidden_units, grad_gate, grad_up = lax.optimization_barrier(
        (passed, hidden_units, grad_gate, grad_up)
    )
    passed = swap(passed, "fsdp", 2)
    grads_shape = ((count // 2, parts * share, block), BF16, True)
    down_kept, down_sent = launch(
        feed_grads_body(parts, count, block, 1),
        [grads_shape] * 2,
        [own_scalar, side_scalar],
        [*feeds, hidden_units],
    )
    down_received = swap(down_sent, "ctx", 1)
    gate_kept, gate_sent, up_kept, up_sent = launch(
        feed_grads_body(parts, count, block, 2),
        [grads_shape] * 4,
        [own_scalar, side_scalar],
        [*feed_inputs, after(grad_gate, down_sent), grad_up],
    )
    passed = after(passed, gate_sent)
    input_far = swap(after(attend_input, passed), "fsdp", 2)

    grad_middle, pack, feed_gain_part, pair_kept, pair_sent = launch(
        back_body(parts, count, half, block),
        [((rows, width), F32), ((3, parts, rows, padded), BF16, True), ((1, width), F32)]
        + [((count // 2, rows, 2 * KEY_WIDTH), BF16)] * 2,
        [own_scalar],
        [
            kept,
            received,
            passed,
            middle,
            feedforward_gain,
            both_rows,
            mixed,
            query,
            log_total,
            early_pos,
            late_pos,
            row_pos,
            cosine,
            sine,
            *key_values,
            *hbm(output_blocks),
        ],
        [
            pltpu.VMEM((count * half, 2 * KEY_WIDTH), BF16),
            pltpu.VMEM((count * half, 2 * KEY_WIDTH), BF16),
        ],
    )

    bits = bits_of("ctx")
    pair_sent, input_near, input_far, hidden_units, down_received = lax.optimization_barrier(
        (pair_sent, attend_input, input_far, hidden_units, down_received)
    )
    pair_received = swap(pair_sent, "ctx", 1)

    def next_step(kept, received, k, *gates):
        received = after(received, *gates)
        total = (kept.astype(F32) + received.astype(F32)).astype(BF16)
        kept, sent = split_side(total, own_ctx, k + 1)
        return kept, sent, swap(sent, "ctx", bits[k + 1])

    def last_step(kept, received, k, *gates):
        received = after(received, *gates)
        for n in range(k, len(bits) - 1):
            kept, _, received = next_step(kept, received, n)
        return (kept.astype(F32) + received.astype(F32))[0]

    pack_far = swap(pack, "fsdp", 2)
    pack_near = swap(pack, "fsdp", 1)
    inputs_swapped = swap(input_near, "fsdp", 1), swap(input_far, "fsdp", 1)
    down_kept, down_sent, down_received = next_step(down_kept, down_received, 0)
    out_kept, out_sent = launch(
        feed_out_body(parts, rows),
        [((2, parts, rows, padded), BF16)] * 2,
        [own_scalar],
        [*down_weights(feed_weights), hidden_units],
    )
    pair_received, pack_far, pack_near, inputs_swapped, out_sent, _ = lax.optimization_barrier(
        (pair_received, pack_far, pack_near, inputs_swapped, out_sent, down_sent)
    )
    gate_received = swap(after(gate_sent, pair_received), "ctx", 1)
    pair_kept, pair_sent = half_step(pair_kept, pair_received)
    pair_received = swap(pair_sent, "ctx", bits[1])
    pack_far, down_received, out_sent, _ = lax.optimization_barrier(
        (pack_far, down_received, out_sent, pair_sent)
    )
    if len(bits) > 2:
        down_kept, down_sent, down_received = next_step(down_kept, down_received, 1)
    packs = [pack, pack_near, pack_far, swap(pack_far, "fsdp", 1)]
    input_all = [attend_input, inputs_swapped[0], input_far, inputs_swapped[1]]
    up_received = swap(after(up_sent, pair_received), "ctx", 1)
    rest_kept, rest_sent = launch(
        attention_grads_body(parts, count, block),
        [((count // 2, 2 * QUERY_WIDTH // count, block), BF16, True)] * 2,
        [own_scalar, side_scalar],
        [*hbm(packs), *hbm(input_all)],
    )
    pair_received, out_now, _ = lax.optimization_barrier((pair_received, out_sent, rest_sent))
    for bit in bits[2:]:
        pair_kept, pair_sent = half_step(pair_kept, pair_received)
        pair_received = swap(pair_sent, "ctx", bit)
    rest_received = swap(after(rest_sent, pair_sent), "ctx", 1)
    pair_received = after(pair_received, down_sent)
    out_received = swap(after(out_now, pair_sent), "fsdp", 1)
    pair_in, input_grad, attention_gain_part = launch(
        input_grad_body(parts, block),
        [((rows, 2 * KEY_WIDTH), BF16), ((width, rows), F32), ((1, width), F32)],
        [own_scalar],
        [
            pair_kept,
            pair_received,
            cosine,
            sine,
            pack,
            both_rows,
            attention_gain,
            grad_middle,
            *hbm(weights),
        ],
        [pltpu.VMEM((parts, rows, block), F32)],
    )
    pair_far = swap(pair_in, "fsdp", 2)
    pair_near = swap(pair_in, "fsdp", 1)
    gains = jnp.concatenate([attention_gain_part, feed_gain_part], axis=0)
    gains = gains + swap(gains, "fsdp", 2)
    gate_kept, gate_part, gate_received = next_step(gate_kept, gate_received, 0, pair_in)
    out_received = after(out_received, pair_in)
    out_passed = (out_kept[1].astype(F32) + out_received[1].astype(F32)).astype(BF16)
    pair_far, gains, _ = lax.optimization_barrier((pair_far, gains, gate_part))
    pair_all = [pair_in, pair_near, pair_far, swap(pair_far, "fsdp", 1)]
    gains = gains + swap(gains, "fsdp", 1)
    up_kept, up_part, up_received = next_step(up_kept, up_received, 0, pair_far)
    pair_all[3], gains, _ = lax.optimization_barrier((pair_all[3], gains, up_part))
    pair_grad_kept, pair_grad_sent = launch(
        pair_grads_body(parts, count, block),
        [((count // 2, 2 * KEY_WIDTH // count, block), BF16)] * 2,
        [own_scalar, side_scalar],
        [*pair_all, *hbm(input_all)],
    )
    gains = after(gains, pair_grad_sent)
    pair_grad_received = swap(pair_grad_sent, "ctx", 1)
    gains_received = swap(gains, "ctx", 1)
    out_passed = swap(after(out_passed, pair_grad_sent), "fsdp", 2)
    gate_part = up_part = pair_grad_sent
    for k in range(1, len(bits) - 1):
        gate_kept, gate_part, gate_received = next_step(gate_kept, gate_received, k, gate_part)
        up_kept, up_part, up_received = next_step(up_kept, up_received, k, gate_part)
    down_own = last_step(down_kept, down_received, min(2, len(bits) - 1), pair_grad_sent)
    for k in range(len(bits) - 1):
        rest_kept, rest_part, rest_received = next_step(
            rest_kept, rest_received, k, pair_grad_sent
        )
        pair_grad_kept, pair_grad_sent, pair_grad_received = next_step(
            pair_grad_kept, pair_grad_received, k, rest_part
        )
        gains = gains + after(gains_received, pair_grad_sent)
        gains_received = swap(gains, "ctx", bits[k + 1])
        pair_grad_received, gains_received, rest_received = lax.optimization_barrier(
            (pair_grad_received, gains_received, rest_received)
        )
    gains = gains + gains_received
    middle = after(middle, up_part)
    gate_own = (gate_kept.astype(F32) + gate_received.astype(F32))[0]
    up_own = (up_kept.astype(F32) + up_received.astype(F32))[0]
    rest_own = (rest_kept.astype(F32) + rest_received.astype(F32))[0]
    pair_own = (pair_grad_kept.astype(F32) + pair_grad_received.astype(F32))[0]
    (block_output,) = launch(
        output_body(parts, block),
        [((width, rows), F32)],
        [],
        [middle, out_kept, out_received, out_passed],
    )
    query_rows, key_rows = QUERY_WIDTH // count, KEY_WIDTH // count
    query_own, output_own = rest_own[:query_rows], rest_own[query_rows:]

    stacked = jnp.concatenate([down_own, gate_own, up_own], axis=0).astype(BF16)
    stacked = stacked.reshape(3, parts, share, block).transpose(1, 0, 2, 3)
    arrived = jnp.stack(exchange_blocks([stacked[j] for j in range(parts)], "fsdp"))
    ordered = jnp.concatenate(
        [lax.dynamic_index_in_dim(arrived, own ^ b, 0, keepdims=False) for b in range(parts)],
        axis=1,
    ).astype(F32)

    return (
        block_output.T[None],
        input_grad.T[None],
        query_own.T[None],
        pair_own[:key_rows].T[None],
        pair_own[key_rows:].T[None],
        output_own[None],
        ordered[1].T[None],
        ordered[2].T[None],
        ordered[0][None],
        gains[:1],
        gains[1:],
    )


def solution(mesh):
    return jax.shard_map(
        shards,
        mesh=mesh,
        in_specs=(
            P("fsdp", "ctx", None),
            P(),
            P(None, "fsdp", None),
            P(None, "fsdp", None),
            P(None, "fsdp", None),
            P(None, None, "fsdp"),
            P(None, "fsdp", None),
            P(None, "fsdp", None),
            P(None, None, "fsdp"),
            P(),
            P(),
            P("fsdp", "ctx", None),
        ),
        out_specs=(
            P("fsdp", "ctx", None),
            P("fsdp", "ctx", None),
            P(None, "fsdp", "ctx"),
            P(None, "fsdp", "ctx"),
            P(None, "fsdp", "ctx"),
            P(None, "ctx", "fsdp"),
            P(None, "fsdp", "ctx"),
            P(None, "fsdp", "ctx"),
            P(None, "ctx", "fsdp"),
            P(),
            P(),
        ),
        check_vma=False,
    )
```
